768 devices in a mesh: dp: 24 (over x, z_hi, core), tensor: 32 (over y, z_lo).
Axes of the slice: x: 4, y: 8, z: 12 (z_hi: 3, z_lo: 4; z = z_hi * 4 + z_lo), core: 2. Of those that a mesh axis runs over, the one named last changes fastest.
Arguments:
- queries: bfloat16 [24, 4, 64, 8192], P('dp', None, None, 'tensor'), may hold values from -64 to 64
- slot_keys_values: bfloat16 [24, 4, 2, 64, 1024], P('dp'), may hold values from -8 to 8
- segment_ids: int32 [24, 4, 64], P('dp'), may hold values from 0 to 3, never falling along the last dimension, each value on 1 to 32 neighbouring positions
- residual_in: bfloat16 [24, 4, 64, 4224], P('dp', None, None, 'tensor'), may hold values from -6 to 6
- cotangent: bfloat16 [24, 4, 64, 4224], P('dp', None, None, 'tensor'), may hold values from -192 to 192
- out_weight: bfloat16 [8192, 4224], P('tensor', 'dp'), may hold values from -0.0625 to 0.0625
- live_mask: int32 [24], replicated, may hold values 0 or 1
- micro_counts: int32 [24], replicated, may hold values from 1 to 4
Outputs:
- block_residual: bfloat16 [24, 4, 64, 4224], P('dp', None, None, 'tensor')
- query_gradient: bfloat16 [24, 4, 64, 8192], P('dp', None, None, 'tensor')
- key_value_grad: bfloat16 [24, 4, 2, 64, 1024], P('dp')
- projection_weight_gradient: float32 [8192, 4224], P('tensor', 'dp')
The draws below stay inside these ranges and needn't reach their ends.
All inputs are finite; a program needn't handle non-finite values.
Results may differ from the reference program's by a relative error of at most 0.014.
Values may be sent and summed in bfloat16 or wider, within the bound.
A program may use at most 64 MiB of HBM per device.

```python
import math
import jax
import jax.numpy as jnp
import numpy as np
from jax import lax

HEAD_SIZE = 128
QUERY_HEADS = 64
KEY_VALUE_HEADS = 8
DW = 4224
SLOT_TOKENS = 64
MICRO_SLOTS = 4
DATA_REPLICAS = 24
N_DP = 24
N_TENSOR = 32


def draw_together(key):
    query_key = jax.random.fold_in(key, 11)
    keyval_key = jax.random.fold_in(key, 12)
    shape_q = (DATA_REPLICAS, MICRO_SLOTS, SLOT_TOKENS, QUERY_HEADS * HEAD_SIZE)
    key_value_shape = (DATA_REPLICAS, MICRO_SLOTS, 2, SLOT_TOKENS, KEY_VALUE_HEADS * HEAD_SIZE)
    query_vals = jax.random.normal(query_key, shape_q, jnp.float32)
    keyval_vals = jax.random.normal(keyval_key, key_value_shape, jnp.float32)
    query_vals = jnp.clip(query_vals, -64.0, 64.0)
    keyval_vals = jnp.clip(keyval_vals, -8.0, 8.0)
    return (query_vals.astype(jnp.bfloat16), keyval_vals.astype(jnp.bfloat16))


def draw_queries(key, part):
    return draw_together(key)[0]


def draw_slot_keys_values(key, part):
    return draw_together(key)[1]


def set_ends(values, own_key, smallest, top_value):
    index_at = [jax.random.randint(jax.random.fold_in(own_key, axis), (), 0, length) for axis, length in enumerate(values.shape)]
    main_axis = values.shape.index(max(values.shape))
    beside = index_at[:main_axis] + [(index_at[main_axis] + 1) % values.shape[main_axis]] + index_at[main_axis + 1:]
    return values.at[tuple(index_at)].set(smallest).at[tuple(beside)].set(top_value)


def spiked(result, stream_key, source, target, blocks, factor):
    def block_of(dim):
        return (jnp.arange(result.shape[dim]) // (result.shape[dim] // blocks)).reshape((-1,) + (1,) * (result.ndim - 1 - dim))

    first = jax.random.permutation(stream_key, blocks)[block_of(target)]
    second = (block_of(target) + blocks // 2) % blocks
    return jnp.where((block_of(source) == first) | (block_of(source) == second), factor * result, result)


def block_levels(key, shape, shards, smallest, top_value):
    def one(position, shards_of):
        draws = jax.random.uniform(jax.random.fold_in(jax.random.fold_in(key, 6), position), (shards_of,), jnp.float32, smallest / len(shards), top_value / len(shards))
        return jnp.repeat(jnp.exp(draws), shape[position] // shards_of).reshape((-1,) + (1,) * (len(shape) - position - 1))

    factor_of = one(*shards[0])
    for cut in shards[1:]:
        factor_of = factor_of * one(*cut)
    return factor_of


def split_up(number_of, total, reach, skew):
    weights = [(1 << 20) // math.isqrt(grade ** skew) + 1 for grade in range(2, number_of + 1)]
    spare, given = total - reach - (number_of - 1), [1] * (number_of - 1)
    while spare > 0:
        candidates = [i for i in range(number_of - 1) if given[i] < reach]
        mass, remaining = sum([weights[i] for i in candidates]), spare
        for i in candidates:
            extra = min(reach - given[i], max(1, remaining * weights[i] // mass), spare)
            given[i] = given[i] + extra
            spare = spare - extra
    return np.array([reach] + given)


def ragged_sizes(rng, amount, total, reach, skew):
    if amount == 2:
        one = jax.random.randint(rng, (), max(1, total - reach), min(reach, total - 1) + 1)
        return jnp.stack([one, total - one])
    tallies = jnp.asarray(split_up(amount, total, reach, skew), jnp.int32)
    twos = (amount - 1) // 2
    source_of, receiver = tallies[1:1 + 2 * twos:2], tallies[2:2 + 2 * twos:2]
    slack = jnp.minimum(source_of - 1, reach - receiver)
    shifted = jax.random.randint(jax.random.fold_in(rng, 1), (twos,), 0, 1 << 20) % (slack + 1)
    tallies = tallies.at[1:1 + 2 * twos:2].set(source_of - shifted).at[2:2 + 2 * twos:2].set(receiver + shifted)
    return tallies[jax.random.permutation(jax.random.fold_in(rng, 2), amount)]


def gaussian(stream_key, shape, scale, reach, pieces=(), kind=jnp.bfloat16):
    level = block_levels(stream_key, shape, pieces, -0.22, 0.18) if pieces else 1.0
    drawn = jax.random.normal(stream_key, shape, jnp.float32) * scale * level
    return jnp.minimum(jnp.maximum(drawn, -reach), reach).astype(kind)


def bell_draw_with(stream_key, extent, spread, reach, pieces, heavy, dtype=jnp.bfloat16):
    result = spread * jax.random.normal(stream_key, extent, jnp.float32)
    if pieces:
        result = result * block_levels(stream_key, extent, pieces, -0.22, 0.18)
    return jnp.clip(spiked(result, jax.random.fold_in(stream_key, 3), *heavy), -reach, reach).astype(dtype)


def setup_inputs(seed: int = 0) -> dict:
    key_of = jax.random.split(jax.random.key(seed), 9)
    return {
        "queries": draw_queries(jax.random.fold_in(key_of[8], 71), 0),
        "slot_keys_values": draw_slot_keys_values(jax.random.fold_in(key_of[8], 71), 0),
        "segment_ids": jax.vmap(lambda own: jnp.searchsorted(jnp.cumsum(ragged_sizes(own, 4, SLOT_TOKENS, SLOT_TOKENS // 2, 1)), jnp.arange(SLOT_TOKENS), side="right"))(jax.random.split(key_of[2], DATA_REPLICAS * MICRO_SLOTS)).reshape((DATA_REPLICAS, MICRO_SLOTS, SLOT_TOKENS)).astype(jnp.int32),
        "residual_in": gaussian(key_of[3], (DATA_REPLICAS, MICRO_SLOTS, SLOT_TOKENS, DW), 1.0, 6.0, ((0, 24), (3, 32))),
        "cotangent": bell_draw_with(key_of[4], (DATA_REPLICAS, MICRO_SLOTS, SLOT_TOKENS, DW), N_DP, 192.0, ((0, 24), (3, 32)), (0, 3, 8, 2.0)),
        "out_weight": gaussian(key_of[5], (QUERY_HEADS * HEAD_SIZE, DW), (QUERY_HEADS * HEAD_SIZE) ** -0.5, 0.0625, ((0, 32), (1, 24))),
        "live_mask": set_ends((jax.random.randint(key_of[6], (DATA_REPLICAS,), 0, 5) < 4).astype(jnp.int32), jax.random.fold_in(key_of[6], 1), 0, 1),
        "micro_counts": set_ends(jax.random.randint(key_of[7], (DATA_REPLICAS,), 1, MICRO_SLOTS + 1), jax.random.fold_in(key_of[7], 1), 1, MICRO_SLOTS).astype(jnp.int32),
    }


def attend_slot(query, key_value_pair, segment):
    heads_per_group = QUERY_HEADS // KEY_VALUE_HEADS
    query_f = query.astype(jnp.float32).reshape(SLOT_TOKENS, QUERY_HEADS, HEAD_SIZE).transpose(1, 0, 2)
    key_value_float = key_value_pair.astype(jnp.float32).reshape(2, SLOT_TOKENS, KEY_VALUE_HEADS, HEAD_SIZE).transpose(0, 2, 1, 3)
    key_f = jnp.repeat(key_value_float[0], heads_per_group, axis=0)
    value_f = jnp.repeat(key_value_float[1], heads_per_group, axis=0)
    positions = jnp.arange(SLOT_TOKENS)
    allowed = (positions[None, :] <= positions[:, None]) & (segment[:, None] == segment[None, :])
    scores = jnp.einsum('hqd,hkd->hqk', query_f, key_f, precision=lax.Precision.HIGHEST) / math.sqrt(HEAD_SIZE)
    masked = jnp.where(allowed[None], scores, -jnp.inf)
    top_score = lax.optimization_barrier(jnp.max(masked, axis=-1, keepdims=True))
    expo = jnp.where(allowed[None], jnp.exp(masked - top_score), 0.0)
    probs = expo / lax.optimization_barrier(jnp.sum(expo, axis=-1, keepdims=True))
    rounded = lax.optimization_barrier(probs.astype(jnp.bfloat16)).astype(jnp.float32)
    context = jnp.einsum('hqk,hkd->qhd', rounded, value_f, precision=lax.Precision.HIGHEST)
    context = context.astype(jnp.bfloat16).reshape(SLOT_TOKENS, QUERY_HEADS * HEAD_SIZE)
    return (context, probs, rounded, query_f, key_f, value_f)

def backward_slot(query, key_value_pair, segment, context_grad):
    context, probs, rounded, query_f, key_f, value_f = attend_slot(query, key_value_pair, segment)
    grad_heads = context_grad.reshape(SLOT_TOKENS, QUERY_HEADS, HEAD_SIZE).transpose(1, 0, 2)
    prob_grad = jnp.einsum('hqd,hkd->hqk', grad_heads, value_f, precision=lax.Precision.HIGHEST)
    delta = lax.optimization_barrier(jnp.sum(prob_grad * probs, axis=-1, keepdims=True))
    score_grad = probs * (prob_grad - delta)
    query_gradient = jnp.einsum('hqk,hkd->qhd', score_grad, key_f, precision=lax.Precision.HIGHEST) / math.sqrt(HEAD_SIZE)
    key_term = jnp.einsum('hqk,hqd->hkd', score_grad, query_f, precision=lax.Precision.HIGHEST) / math.sqrt(HEAD_SIZE)
    value_term = jnp.einsum('hqk,hqd->hkd', rounded, grad_heads, precision=lax.Precision.HIGHEST)
    addend_terms = jnp.stack([key_term, value_term], axis=0)
    addend_terms = lax.optimization_barrier(addend_terms.astype(jnp.bfloat16)).astype(jnp.float32)
    reduced_total = addend_terms.reshape(2, KEY_VALUE_HEADS, QUERY_HEADS // KEY_VALUE_HEADS, SLOT_TOKENS, HEAD_SIZE).sum(axis=2)
    key_value_gradient = reduced_total.transpose(0, 2, 1, 3).reshape(2, SLOT_TOKENS, KEY_VALUE_HEADS * HEAD_SIZE).astype(jnp.bfloat16)
    return (query_gradient.reshape(SLOT_TOKENS, QUERY_HEADS * HEAD_SIZE).astype(jnp.bfloat16), key_value_gradient)

def reference(queries, slot_keys_values, segment_ids, residual_in, cotangent, out_weight, live_mask, micro_counts):
    slot_entries = DATA_REPLICAS * MICRO_SLOTS
    query_flat = queries.reshape(slot_entries, SLOT_TOKENS, QUERY_HEADS * HEAD_SIZE)
    key_value_flattened = slot_keys_values.reshape(slot_entries, 2, SLOT_TOKENS, KEY_VALUE_HEADS * HEAD_SIZE)
    segment_flat = segment_ids.reshape(slot_entries, SLOT_TOKENS)
    context = lax.map(lambda ops: attend_slot(ops[0], ops[1], ops[2])[0], (query_flat, key_value_flattened, segment_flat))
    heads_here = QUERY_HEADS // N_TENSOR
    context_rows = context.reshape(slot_entries * SLOT_TOKENS, N_TENSOR, heads_here * HEAD_SIZE).transpose(1, 0, 2)
    weight_groups = out_weight.reshape(N_TENSOR, heads_here * HEAD_SIZE, DW)

    def add_group(running, group_idx):
        term = jnp.dot(context_rows[group_idx], weight_groups[group_idx], preferred_element_type=jnp.float32)
        term = lax.optimization_barrier(term.astype(jnp.bfloat16)).astype(jnp.float32)
        return (running + term, None)
    reduced_total, _ = lax.scan(add_group, jnp.zeros((slot_entries * SLOT_TOKENS, DW), jnp.float32), jnp.arange(N_TENSOR))
    block_residual = (residual_in.astype(jnp.float32) + reduced_total.reshape(DATA_REPLICAS, MICRO_SLOTS, SLOT_TOKENS, DW)).astype(jnp.bfloat16)
    live_total = jnp.maximum(jnp.sum(live_mask * micro_counts), 1)
    slot_live = (jnp.arange(MICRO_SLOTS)[None, :] < micro_counts[:, None]) & (live_mask[:, None] > 0)
    slot_weight = slot_live.astype(jnp.float32) / live_total.astype(jnp.float32)
    scaled_cot = (cotangent.astype(jnp.float32) * slot_weight[:, :, None, None]).astype(jnp.bfloat16)
    cot_rows = scaled_cot.reshape(slot_entries * SLOT_TOKENS, DW)
    context_grad = jnp.dot(cot_rows, out_weight.T, preferred_element_type=jnp.float32)
    projection_weight_gradient = jnp.dot(context.reshape(slot_entries * SLOT_TOKENS, QUERY_HEADS * HEAD_SIZE).T, cot_rows, preferred_element_type=jnp.float32)
    query_gradient, key_value_gradient = lax.map(lambda ops: backward_slot(ops[0], ops[1], ops[2], ops[3]), (query_flat, key_value_flattened, segment_flat, context_grad.reshape(slot_entries, SLOT_TOKENS, QUERY_HEADS * HEAD_SIZE)))
    return (block_residual, query_gradient.reshape(DATA_REPLICAS, MICRO_SLOTS, SLOT_TOKENS, QUERY_HEADS * HEAD_SIZE), key_value_gradient.reshape(DATA_REPLICAS, MICRO_SLOTS, 2, SLOT_TOKENS, KEY_VALUE_HEADS * HEAD_SIZE), projection_weight_gradient)
```

```python
import math

import jax
import jax.numpy as jnp
from jax import lax
from jax.experimental import pallas as pl
from jax.experimental.pallas import tpu as pltpu
from jax.sharding import PartitionSpec as P

HEAD_SIZE = 128
MESH = pl.DeviceIdType.MESH
F32 = jnp.float32
BF16 = jnp.bfloat16

BLOCKS = 96
REAL = 44
ROWS = 48
C_BLOCKS = 3
W_BLOCKS = 4
TOKENS = 256
N_SEND = 176


def dot(a, b, ca, cb):
    return lax.dot_general(a, b, (((ca,), (cb,)), ((), ())), preferred_element_type=F32)


def kernel(
    c_own, w_own, q_ref, kv_hbm, seg_col, seg_row,
    o_res, o_q, o_kv, o_w,
    cg, wg, po, rp, rm, fz, cz, e_send, e_core, es, ex0, ex1, ex2, fe, ez,
    d_own, dz, kvs, ctx, probs, dctx,
    ssem, bsem, asem, rpsem, rmsem, czsem, ecsem, exsem, ezsem, dzsem, kvsem, ldsem,
):
    dpi = lax.axis_index("dp")
    ti = lax.axis_index("tensor")
    core = lax.rem(dpi, 2)
    zh = lax.rem(lax.div(dpi, 2), 3)
    x = lax.div(dpi, 6)
    zl = lax.rem(ti, 4)
    y = lax.div(ti, 4)
    way = 1 - 2 * core

    def y_at(k):
        return lax.rem(y + (k + 8), 8)

    def x_at(k):
        return lax.rem(x + k + 4, 4)

    zlj = [zl, zl + 1 - 2 * lax.rem(zl, 2), lax.rem(zl + 2, 4), 3 - zl]
    zhk = [zh, lax.rem(zh + 1, 3), lax.rem(zh + 2, 3)]
    on_y = {k: (dpi, y_at(k) * 4 + zl) for k in (1, -1)}
    on_zl = [None] + [(dpi, y * 4 + zlj[j]) for j in (1, 2, 3)]
    on_zh = [None] + [((x * 3 + zhk[k]) * 2 + core, ti) for k in (1, 2)]
    on_x = {k: ((x_at(k * way) * 3 + zh) * 2 + core, ti) for k in (1, -1)}
    other = (dpi + way, ti)

    sends = []

    def send(src, dst, sem, device):
        copy = pltpu.make_async_remote_copy(
            src_ref=src, dst_ref=dst, send_sem=ssem.at[len(sends)], recv_sem=sem,
            device_id=device, device_id_type=MESH,
        )
        copy.start()
        sends.append(copy)

    def arrive(dst, sem):
        pltpu.make_async_remote_copy(
            src_ref=dst, dst_ref=dst, send_sem=ssem.at[0], recv_sem=sem,
            device_id=other, device_id_type=MESH,
        ).wait_recv()

    partners = [on_y[1], on_y[-1], *on_zl[1:], *on_zh[1:], on_x[1], on_x[-1], other]
    barrier = pltpu.get_barrier_semaphore()
    for partner in partners:
        pl.semaphore_signal(barrier, inc=1, device_id=partner, device_id_type=MESH)

    load = pltpu.make_async_copy(
        kv_hbm.at[:, :, :, pl.ds(pl.multiple_of(y * HEAD_SIZE, HEAD_SIZE), HEAD_SIZE)], kvs, ldsem
    )
    load.start()

    def c_at(buf, t):
        return buf.at[pl.ds(t * C_BLOCKS, C_BLOCKS)]

    def w_at(buf, d):
        return buf.at[pl.ds(d * W_BLOCKS, W_BLOCKS)]

    cg[pl.ds(ti * C_BLOCKS, C_BLOCKS)] = c_own[...]
    wg[pl.ds(dpi * W_BLOCKS, W_BLOCKS)] = w_own[...]
    load.wait()

    scale = 1.0 / math.sqrt(HEAD_SIZE)

    def attend(head):
        cols = slice(head * HEAD_SIZE, (head + 1) * HEAD_SIZE)
        key = kvs[:, 0].reshape(TOKENS, HEAD_SIZE)
        value = kvs[:, 1].reshape(TOKENS, HEAD_SIZE)
        scores = dot(q_ref[:, cols], key, 1, 1) * scale
        row = lax.broadcasted_iota(jnp.int32, (TOKENS, TOKENS), 0)
        col = lax.broadcasted_iota(jnp.int32, (TOKENS, TOKENS), 1)
        allowed = (col <= row) & (seg_col[...] == seg_row[...])
        scores = jnp.where(allowed, scores, -1e30)
        top = jnp.max(scores, axis=1, keepdims=True)
        expo = jnp.where(allowed, jnp.exp(scores - top), 0.0)
        p = expo / jnp.sum(expo, axis=1, keepdims=True)
        probs[head] = p
        ctx[:, cols] = dot(p.astype(BF16), value, 1, 0).astype(BF16)

    attend(0)
    pl.semaphore_wait(barrier, len(partners))

    def gather_sends(own, place, sem):
        for k in (1, -1):
            send(own, place(ti), sem.at[ti], on_y[k])
        for j in (1, 2, 3):
            send(own, place(ti), sem.at[ti], on_zl[j])

    def gather_step(place, sem, s, j):
        if s == 0:
            t = y * 4 + zlj[j]
            arrive(place(t), sem.at[t])
            for k in (1, -1):
                send(place(t), place(t), sem.at[t], on_y[k])
            return
        for k, mine in ((1, j < 2), (-1, j >= 2)):
            if s == 4 and not mine:
                continue
            t = y_at(-k * s) * 4 + zlj[j]
            arrive(place(t), sem.at[t])
            if s < 3 or (s == 3 and mine):
                send(place(t), place(t), sem.at[t], on_y[k])

    steps = {n: [] for n in range(1, 8)}
    for s in (4, 3, 2, 1, 0):
        for j in range(4):
            if s + j > 0:
                steps[s + j].append((s, j))

    def c_place(t):
        return c_at(cg, t)

    def w_x(k, d_x, zhx, forward):
        d = (d_x * 3 + zhx) * 2 + core
        arrive(w_at(wg, d), asem.at[d])
        if forward:
            send(w_at(wg, d), w_at(wg, d), asem.at[d], on_x[k])
        send(w_at(wg, d), w_at(wg, d), asem.at[d], other)

    def w_x_all(zhx):
        w_x(1, x_at(-way), zhx, True)
        w_x(1, x_at(way), zhx, False)
        w_x(1, x_at(2), zhx, False)

    gather_sends(c_own, c_place, bsem)
    for k in (1, -1):
        send(w_own, w_at(wg, dpi), asem.at[dpi], on_x[k])
    send(w_own, w_at(wg, dpi), asem.at[dpi], other)

    def run_steps(n):
        for s, j in steps[n]:
            gather_step(c_place, bsem, s, j)

    run_steps(1)
    for k in (1, 2):
        send(w_own, w_at(wg, dpi), asem.at[dpi], on_zh[k])
    attend(1)
    run_steps(2)
    w_x_all(zh)
    run_steps(3)
    run_steps(4)
    for k in (1, 2):
        d = (x * 3 + zhk[k]) * 2 + core
        arrive(w_at(wg, d), asem.at[d])
        for m in (1, -1):
            send(w_at(wg, d), w_at(wg, d), asem.at[d], on_x[m])
        send(w_at(wg, d), w_at(wg, d), asem.at[d], other)
    run_steps(5)
    w_x_all(zhk[1])
    run_steps(6)
    w_x_all(zhk[2])
    for xd in range(4):
        for zd in range(3):
            d = (xd * 3 + zd) * 2 + 1 - core
            arrive(w_at(wg, d), asem.at[d])

    def project(i, carry):
        n = 8
        out = dot(wg[pl.ds(i * n, n)].reshape(n * ROWS, TOKENS), ctx[...], 1, 1)
        po[pl.ds(i * n, n)] = out.astype(BF16).reshape(n, ROWS, TOKENS)
        return carry

    lax.fori_loop(0, BLOCKS // 8, project, 0)

    recv_buf = {1: (rp, rpsem), -1: (rm, rmsem)}

    def p_at(k, j):
        return c_at(po, y_at(k) * 4 + zlj[j])

    def slot(k, r, j):
        buf, sem = recv_buf[k]
        i = (r - 1) * 4 + j
        return buf.at[i], sem.at[i]

    def starts(k, j):
        return (j < 2) if k == 1 else (j >= 2)

    def ring_first():
        for j in range(4):
            for k in (1, -1):
                if starts(k, j):
                    send(p_at(4, j), *slot(k, 1, j), on_y[k])
        for j in range(4):
            for k in (1, -1):
                if not starts(k, j):
                    send(p_at(3 * k, j), *slot(k, 2, j), on_y[k])

    def ring_step(r):
        for j in range(4):
            for k in (1, -1):
                if r == 1 and not starts(k, j):
                    continue
                buf, sem = slot(k, r, j)
                arrive(buf, sem)
                own = po[pl.ds((y_at(k * (4 - r)) * 4 + zlj[j]) * C_BLOCKS, C_BLOCKS)]
                buf[...] = (buf[...].astype(F32) + own.astype(F32)).astype(BF16)
                send(buf, *slot(k, r + 1, j), on_y[k])

    ring_first()
    run_steps(7)

    def grad_chunk(d):
        return dot(cg[pl.ds(d * W_BLOCKS, W_BLOCKS)].reshape(W_BLOCKS * ROWS, TOKENS), ctx[...], 1, 0)

    for xd in (x_at(2), x_at(way), x_at(-way), x):
        for zd in range(3):
            c12 = xd * 3 + zd
            part = grad_chunk(c12 * 2 + 1 - core).astype(BF16)
            e_send[c12] = part.reshape(W_BLOCKS, ROWS, TOKENS)
            send(e_send.at[c12], e_core.at[c12], ecsem.at[c12], other)

    ring_step(1)

    dctx[...] = jnp.zeros_like(dctx)

    def back(i, carry):
        n = 16
        dctx[...] += dot(
            cg[pl.ds(i * n, n)].reshape(n * ROWS, TOKENS),
            wg[pl.ds(i * n, n)].reshape(n * ROWS, TOKENS), 0, 0,
        )
        return carry

    lax.fori_loop(0, BLOCKS // 16, back, 0)
    ring_step(2)

    def attend_back(head):
        cols = slice(head * HEAD_SIZE, (head + 1) * HEAD_SIZE)
        key = kvs[:, 0].reshape(TOKENS, HEAD_SIZE)
        value = kvs[:, 1].reshape(TOKENS, HEAD_SIZE)
        grad = dctx[:, cols].astype(BF16)
        p = probs[head]
        prob_grad = dot(grad, value, 1, 1)
        delta = jnp.sum(prob_grad * p, axis=1, keepdims=True)
        score_grad = (p * (prob_grad - delta)).astype(BF16)
        o_q[:, cols] = (dot(score_grad, key, 1, 0) * scale).astype(BF16)
        return dot(score_grad, q_ref[:, cols], 0, 0) * scale, dot(p.astype(BF16), grad, 0, 0)

    key_a, value_a = attend_back(0)
    key_b, value_b = attend_back(1)
    d_own[:, 0] = (key_a + key_b).astype(BF16).reshape(4, 64, HEAD_SIZE)
    d_own[:, 1] = (value_a + value_b).astype(BF16).reshape(4, 64, HEAD_SIZE)
    for j in (1, 2, 3):
        send(d_own.at[zlj[j]], dz.at[j], dzsem.at[j], on_zl[j])

    def grad_sum(xd):
        for zd in range(3):
            c12 = xd * 3 + zd
            part = grad_chunk(c12 * 2 + core)
            arrive(e_core.at[c12], ecsem.at[c12])
            part = part.reshape(W_BLOCKS, ROWS, TOKENS) + e_core[c12].astype(F32)
            es[c12] = part.astype(BF16)

    grad_sum(x_at(2))
    for zd in range(3):
        send(es.at[x_at(2) * 3 + zd], ex0.at[zd], exsem.at[zd], on_x[1])
    grad_sum(x_at(-way))
    for zd in range(3):
        send(es.at[x_at(-way) * 3 + zd], ex2.at[zd], exsem.at[6 + zd], on_x[-1])
    ring_step(3)

    def kv_place(t):
        lanes = pl.ds(pl.multiple_of(lax.div(t, 4) * HEAD_SIZE, HEAD_SIZE), HEAD_SIZE)
        return o_kv.at[lax.rem(t, 4), :, :, lanes]

    total = d_own[zl].astype(F32)
    for j in (1, 2, 3):
        arrive(dz.at[j], dzsem.at[j])
        total = total + dz[j].astype(F32)
    d_sum = total.astype(BF16)
    dz[0] = d_sum
    o_kv[zl, :, :, pl.ds(pl.multiple_of(y * HEAD_SIZE, HEAD_SIZE), HEAD_SIZE)] = d_sum
    gather_sends(dz.at[0], kv_place, kvsem)

    grad_sum(x_at(way))
    for zd in range(3):
        c12 = x_at(way) * 3 + zd
        arrive(ex0.at[zd], exsem.at[zd])
        ex0[zd] = (ex0[zd].astype(F32) + es[c12].astype(F32)).astype(BF16)
        send(ex0.at[zd], ex1.at[zd], exsem.at[3 + zd], on_x[1])

    mine = None
    for j in (1, 2, 3, 0):
        acc = po[pl.ds((y * 4 + zlj[j]) * C_BLOCKS, C_BLOCKS)].astype(F32)
        for k in (1, -1):
            buf, sem = slot(k, 4, j)
            arrive(buf, sem)
            acc = acc + buf[...].astype(F32)
        if j:
            fz[j] = acc.astype(BF16)
            send(fz.at[j], cz.at[j], czsem.at[j], on_zl[j])
        else:
            o_res[...] = acc

    for n in (1, 2, 3):
        for s, j in steps[n]:
            gather_step(kv_place, kvsem, s, j)

    grad_sum(x)
    for zd in range(3):
        arrive(ex1.at[zd], exsem.at[3 + zd])
        arrive(ex2.at[zd], exsem.at[6 + zd])

    def arrived(zd):
        return es[x * 3 + zd].astype(F32) + ex1[zd].astype(F32) + ex2[zd].astype(F32)

    for k in (1, 2):
        fe[k] = arrived(zhk[k]).astype(BF16)
        send(fe.at[k], ez.at[k], ezsem.at[k], on_zh[k])
    o_w[...] = arrived(zh)

    for n in (4, 5, 6):
        for s, j in steps[n]:
            gather_step(kv_place, kvsem, s, j)
    for j in (1, 2, 3):
        arrive(cz.at[j], czsem.at[j])
        o_res[...] += cz[j].astype(F32)
    for k in (1, 2):
        arrive(ez.at[k], ezsem.at[k])
        o_w[...] += ez[k].astype(F32)
    for s, j in steps[7]:
        gather_step(kv_place, kvsem, s, j)

    for copy in sends:
        copy.wait_send()


def exchange(c_own, w_own, q, kv, seg_col, seg_row):
    c_shape = (C_BLOCKS, ROWS, TOKENS)
    w_shape = (W_BLOCKS, ROWS, TOKENS)
    vmem = pl.BlockSpec(memory_space=pltpu.VMEM)
    dma = pltpu.SemaphoreType.DMA
    return pl.pallas_call(
        kernel,
        out_shape=(
            jax.ShapeDtypeStruct(c_shape, F32),
            jax.ShapeDtypeStruct((TOKENS, TOKENS), BF16),
            jax.ShapeDtypeStruct(kv.shape, BF16),
            jax.ShapeDtypeStruct(w_shape, F32),
        ),
        in_specs=[vmem, vmem, vmem, pl.BlockSpec(memory_space=pl.ANY), vmem, vmem],
        out_specs=(vmem, vmem, vmem, vmem),
        scratch_shapes=[
            pltpu.VMEM((BLOCKS, ROWS, TOKENS), BF16),
            pltpu.VMEM((BLOCKS, ROWS, TOKENS), BF16),
            pltpu.VMEM((BLOCKS, ROWS, TOKENS), BF16),
            pltpu.VMEM((16, *c_shape), BF16),
            pltpu.VMEM((16, *c_shape), BF16),
            pltpu.VMEM((4, *c_shape), BF16),
            pltpu.VMEM((4, *c_shape), BF16),
            pltpu.VMEM((12, *w_shape), BF16),
            pltpu.VMEM((12, *w_shape), BF16),
            pltpu.VMEM((12, *w_shape), BF16),
            pltpu.VMEM((3, *w_shape), BF16),
            pltpu.VMEM((3, *w_shape), BF16),
            pltpu.VMEM((3, *w_shape), BF16),
            pltpu.VMEM((3, *w_shape), BF16),
            pltpu.VMEM((3, *w_shape), BF16),
            pltpu.VMEM((4, 2, 64, HEAD_SIZE), BF16),
            pltpu.VMEM((4, 2, 64, HEAD_SIZE), BF16),
            pltpu.VMEM((4, 2, 64, HEAD_SIZE), BF16),
            pltpu.VMEM((TOKENS, TOKENS), BF16),
            pltpu.VMEM((2, TOKENS, TOKENS), F32),
            pltpu.VMEM((TOKENS, TOKENS), F32),
            dma((N_SEND,)),
            dma((32,)),
            dma((24,)),
            dma((16,)),
            dma((16,)),
            dma((4,)),
            dma((12,)),
            dma((9,)),
            dma((3,)),
            dma((4,)),
            dma((32,)),
            dma(()),
        ],
        compiler_params=pltpu.CompilerParams(
            collective_id=0, has_side_effects=True, vmem_limit_bytes=48 * 1024 * 1024
        ),
    )(c_own, w_own, q, kv, seg_col, seg_row)


def padded(rows, blocks):
    return jnp.pad(rows.reshape(blocks, REAL, TOKENS), ((0, 0), (0, ROWS - REAL), (0, 0)))


def per_device(
    queries, slot_keys_values, segment_ids, residual_in, cotangent, out_weight, live_mask, micro_counts
):
    replica = lax.axis_index("dp")
    slots = queries.shape[1]
    pick = jnp.arange(live_mask.shape[0]) == replica
    my_live = jnp.sum(jnp.where(pick, live_mask, 0))
    my_count = jnp.sum(jnp.where(pick, micro_counts, 0))
    live_total = jnp.maximum(jnp.sum(live_mask * micro_counts), 1)
    slot_live = (jnp.arange(slots) < my_count) & (my_live > 0)
    slot_weight = slot_live.astype(F32) / live_total.astype(F32)
    scaled = (cotangent[0].astype(F32) * slot_weight[:, None, None]).astype(BF16)
    c_own = padded(scaled.reshape(TOKENS, -1).T, C_BLOCKS)
    w_own = padded(out_weight.T, W_BLOCKS)
    seg = (segment_ids[0] + 8 * jnp.arange(slots)[:, None]).reshape(TOKENS)
    res, q_grad, kv_grad, w_grad = exchange(
        c_own, w_own, queries[0].reshape(TOKENS, TOKENS), slot_keys_values[0],
        seg.reshape(TOKENS, 1), seg.reshape(1, TOKENS),
    )
    total = res[:, :REAL].reshape(C_BLOCKS * REAL, TOKENS).T.reshape(residual_in.shape)
    block_residual = (residual_in.astype(F32) + total).astype(BF16)
    w_grad = w_grad[:, :REAL].reshape(W_BLOCKS * REAL, TOKENS).T
    return (block_residual, q_grad.reshape(queries.shape), kv_grad[None], w_grad)


def solution(mesh):
    placed = (
        P("dp", None, None, "tensor"),
        P("dp", None, None, None, None),
        P("dp", None, None),
        P("dp", None, None, "tensor"),
        P("dp", None, None, "tensor"),
        P("tensor", "dp"),
        P(),
        P(),
    )
    return jax.shard_map(
        per_device,
        mesh=mesh,
        in_specs=placed,
        out_specs=(
            P("dp", None, None, "tensor"),
            P("dp", None, None, "tensor"),
            P("dp", None, None, None, None),
            P("tensor", "dp"),
        ),
        check_vma=False,
    )
```

```python
import math

import jax
import jax.numpy as jnp
from jax import lax
from jax.experimental import pallas as pl
from jax.experimental.pallas import tpu as pltpu
from jax.sharding import PartitionSpec as P

HEAD_SIZE = 128
MESH = pl.DeviceIdType.MESH
F32 = jnp.float32
BF16 = jnp.bfloat16

BLOCKS = 96
REAL = 44
ROWS = 48
C_BLOCKS = 3
W_BLOCKS = 4
TOKENS = 256
N_SEND = 176


def dot(a, b, ca, cb):
    return lax.dot_general(a, b, (((ca,), (cb,)), ((), ())), preferred_element_type=F32)


def one_hot(rows, cols):
    row = lax.broadcasted_iota(jnp.int32, (rows, cols), 0)
    col = lax.broadcasted_iota(jnp.int32, (rows, cols), 1)
    offset = lax.rem(row, ROWS)
    return jnp.where((col == lax.div(row, ROWS) * REAL + offset) & (offset < REAL), 1.0, 0.0).astype(BF16)


def kernel(
    cot_ref, w_ref, q_ref, kv_hbm, seg_ref, res_ref, live_ref, count_ref,
    o_res, o_q, o_kv, o_w,
    c_own, w_own, cg, wg, po, rp, rm, fz, cz, e_send, e_core, es, ex0, ex1, ex2, fe, ez,
    d_own, dz, kvs, ctx, bias, probs, dctx,
    ssem, bsem, asem, rpsem, rmsem, czsem, ecsem, exsem, ezsem, dzsem, kvsem, ldsem,
):
    dpi = lax.axis_index("dp")
    ti = lax.axis_index("tensor")
    core = lax.rem(dpi, 2)
    zh = lax.rem(lax.div(dpi, 2), 3)
    x = lax.div(dpi, 6)
    zl = lax.rem(ti, 4)
    y = lax.div(ti, 4)
    way = 1 - 2 * core

    def y_at(k):
        return lax.rem(y + (k + 8), 8)

    def x_at(k):
        return lax.rem(x + k + 4, 4)

    zlj = [zl, zl + 1 - 2 * lax.rem(zl, 2), lax.rem(zl + 2, 4), 3 - zl]
    zhk = [zh, lax.rem(zh + 1, 3), lax.rem(zh + 2, 3)]
    on_y = {k: (dpi, y_at(k) * 4 + zl) for k in (1, -1)}
    on_zl = [None] + [(dpi, y * 4 + zlj[j]) for j in (1, 2, 3)]
    on_zh = [None] + [((x * 3 + zhk[k]) * 2 + core, ti) for k in (1, 2)]
    on_x = {k: ((x_at(k * way) * 3 + zh) * 2 + core, ti) for k in (1, -1)}
    other = (dpi + way, ti)

    sends = []

    def send(src, dst, sem, device):
        copy = pltpu.make_async_remote_copy(
            src_ref=src, dst_ref=dst, send_sem=ssem.at[len(sends)], recv_sem=sem,
            device_id=device, device_id_type=MESH,
        )
        copy.start()
        sends.append(copy)

    def arrive(dst, sem):
        pltpu.make_async_remote_copy(
            src_ref=dst, dst_ref=dst, send_sem=ssem.at[0], recv_sem=sem,
            device_id=other, device_id_type=MESH,
        ).wait_recv()

    partners = [on_y[1], on_y[-1], *on_zl[1:], *on_zh[1:], on_x[1], on_x[-1], other]
    barrier = pltpu.get_barrier_semaphore()
    for partner in partners:
        pl.semaphore_signal(barrier, inc=1, device_id=partner, device_id_type=MESH)

    load = pltpu.make_async_copy(
        kv_hbm.at[:, :, :, pl.ds(pl.multiple_of(y * HEAD_SIZE, HEAD_SIZE), HEAD_SIZE)], kvs, ldsem
    )
    load.start()

    units = 0
    for r in range(live_ref.shape[0]):
        units = units + live_ref[r] * count_ref[r]
    slot = lax.div(lax.broadcasted_iota(jnp.int32, (TOKENS, 1), 0), 64)
    counted = jnp.where(slot < count_ref[dpi], 1, 0) * jnp.where(live_ref[dpi] > 0, 1, 0)
    weight = counted.astype(F32) / jnp.full((TOKENS, 1), jnp.maximum(units, 1), jnp.int32).astype(F32)
    scaled = (cot_ref[...].astype(F32) * weight).astype(BF16)
    c_hot = one_hot(C_BLOCKS * ROWS, cot_ref.shape[1])
    c_block = dot(c_hot, scaled, 1, 1).astype(BF16).reshape(C_BLOCKS, ROWS, TOKENS)
    c_own[...] = c_block
    cg[pl.ds(ti * C_BLOCKS, C_BLOCKS)] = c_block
    w_block = dot(one_hot(W_BLOCKS * ROWS, w_ref.shape[0]), w_ref[...], 1, 0)
    w_block = w_block.astype(BF16).reshape(W_BLOCKS, ROWS, TOKENS)
    w_own[...] = w_block
    wg[pl.ds(dpi * W_BLOCKS, W_BLOCKS)] = w_block

    def c_place(t):
        return cg.at[pl.ds(t * C_BLOCKS, C_BLOCKS)]

    def w_place(d):
        return wg.at[pl.ds(d * W_BLOCKS, W_BLOCKS)]

    scale = 1.0 / math.sqrt(HEAD_SIZE)

    def mask():
        row = lax.broadcasted_iota(jnp.int32, (TOKENS, TOKENS), 0)
        col = lax.broadcasted_iota(jnp.int32, (TOKENS, TOKENS), 1)
        at = lax.broadcasted_iota(jnp.int32, (64, TOKENS), 0)
        token = lax.broadcasted_iota(jnp.int32, (64, TOKENS), 1)
        tile = jnp.where(lax.rem(token, 64) == at, 1.0, 0.0).astype(BF16)
        seg = seg_ref[...].astype(F32).astype(BF16)
        across = dot(seg, tile, 1, 0)
        down = dot(tile, seg, 0, 1)
        keep = lax.div(lax.broadcasted_iota(jnp.int32, (4, TOKENS), 1), 64)
        keep = keep == lax.broadcasted_iota(jnp.int32, (4, TOKENS), 0)
        seg_row = jnp.sum(jnp.where(keep, across, 0.0), axis=0, keepdims=True)
        keep = lax.div(lax.broadcasted_iota(jnp.int32, (TOKENS, 4), 0), 64)
        keep = keep == lax.broadcasted_iota(jnp.int32, (TOKENS, 4), 1)
        seg_col = jnp.sum(jnp.where(keep, down, 0.0), axis=1, keepdims=True)
        allowed = (col <= row) & (lax.div(col, 64) == lax.div(row, 64)) & (seg_col == seg_row)
        bias[...] = jnp.where(allowed, 0.0, -1e30)

    def attend(head):
        cols = slice(head * HEAD_SIZE, (head + 1) * HEAD_SIZE)
        key = kvs[:, 0].reshape(TOKENS, HEAD_SIZE)
        value = kvs[:, 1].reshape(TOKENS, HEAD_SIZE)
        scores = dot(q_ref[:, cols], key, 1, 1) * scale + bias[...]
        top = jnp.max(scores, axis=1, keepdims=True)
        expo = jnp.exp(scores - top)
        p = expo / jnp.sum(expo, axis=1, keepdims=True)
        probs[head] = p
        ctx[:, cols] = dot(p.astype(BF16), value, 1, 0).astype(BF16)

    def gather_step(place, sem, s, j):
        if s == 0:
            t = y * 4 + zlj[j]
            arrive(place(t), sem.at[t])
            for k in (1, -1):
                send(place(t), place(t), sem.at[t], on_y[k])
            return
        for k, mine in ((1, j < 2), (-1, j >= 2)):
            if s == 4 and not mine:
                continue
            t = y_at(-k * s) * 4 + zlj[j]
            arrive(place(t), sem.at[t])
            if s < 3 or (s == 3 and mine):
                send(place(t), place(t), sem.at[t], on_y[k])

    steps = {n: [] for n in range(1, 11)}
    for s in (4, 3, 2, 1, 0):
        for j in range(4):
            if s + j > 0:
                steps[s + 2 * j].append((s, j))

    def c_steps(*ns):
        for n in ns:
            for s, j in steps[n]:
                gather_step(c_place, bsem, s, j)

    def w_x(d_x, zhx, forward):
        d = (d_x * 3 + zhx) * 2 + core
        arrive(w_place(d), asem.at[d])
        if forward:
            send(w_place(d), w_place(d), asem.at[d], on_x[1])
        send(w_place(d), w_place(d), asem.at[d], other)

    def w_x_all(zhx):
        w_x(x_at(-way), zhx, True)
        w_x(x_at(way), zhx, False)
        w_x(x_at(2), zhx, False)

    def project(i, carry):
        n = 8
        out = dot(wg[pl.ds(i * n, n)].reshape(n * ROWS, TOKENS), ctx[...], 1, 1)
        po[pl.ds(i * n, n)] = out.astype(BF16).reshape(n, ROWS, TOKENS)
        return carry

    recv_buf = {1: (rp, rpsem), -1: (rm, rmsem)}

    def p_at(k, j):
        return po.at[pl.ds((y_at(k) * 4 + zlj[j]) * C_BLOCKS, C_BLOCKS)]

    def ring_slot(k, r, j):
        buf, sem = recv_buf[k]
        i = (r - 1) * 4 + j
        return buf.at[i], sem.at[i]

    def starts(k, j):
        return (j < 2) if k == 1 else (j >= 2)

    def ring_first():
        for j in range(4):
            for k in (1, -1):
                if starts(k, j):
                    send(p_at(4, j), *ring_slot(k, 1, j), on_y[k])
        for j in range(4):
            for k in (1, -1):
                if not starts(k, j):
                    send(p_at(3 * k, j), *ring_slot(k, 2, j), on_y[k])

    def ring_step(r):
        for j in range(4):
            for k in (1, -1):
                if r == 1 and not starts(k, j):
                    continue
                buf, _ = recv_buf[k]
                i = (r - 1) * 4 + j
                arrive(*ring_slot(k, r, j))
                own = po[pl.ds((y_at(k * (4 - r)) * 4 + zlj[j]) * C_BLOCKS, C_BLOCKS)]
                buf[i] = (buf[i].astype(F32) + own.astype(F32)).astype(BF16)
                send(ring_slot(k, r, j)[0], *ring_slot(k, r + 1, j), on_y[k])

    def ring_last(j):
        acc = po[pl.ds((y * 4 + zlj[j]) * C_BLOCKS, C_BLOCKS)].astype(F32)
        for k in (1, -1):
            arrive(*ring_slot(k, 4, j))
            acc = acc + recv_buf[k][0][12 + j].astype(F32)
        return acc

    def grad_chunk(d):
        return dot(cg[pl.ds(d * W_BLOCKS, W_BLOCKS)].reshape(W_BLOCKS * ROWS, TOKENS), ctx[...], 1, 0)

    def grad_share(xd):
        for zd in range(3):
            c12 = xd * 3 + zd
            part = grad_chunk(c12 * 2 + 1 - core).astype(BF16)
            e_send[c12] = part.reshape(W_BLOCKS, ROWS, TOKENS)
            send(e_send.at[c12], e_core.at[c12], ecsem.at[c12], other)

    def grad_sum(xd):
        for zd in range(3):
            c12 = xd * 3 + zd
            part = grad_chunk(c12 * 2 + core)
            arrive(e_core.at[c12], ecsem.at[c12])
            part = part.reshape(W_BLOCKS, ROWS, TOKENS) + e_core[c12].astype(F32)
            es[c12] = part.astype(BF16)

    def back(i, carry):
        n = 16
        dctx[...] += dot(
            cg[pl.ds(i * n, n)].reshape(n * ROWS, TOKENS),
            wg[pl.ds(i * n, n)].reshape(n * ROWS, TOKENS), 0, 0,
        )
        return carry

    def attend_back(head):
        cols = slice(head * HEAD_SIZE, (head + 1) * HEAD_SIZE)
        key = kvs[:, 0].reshape(TOKENS, HEAD_SIZE)
        value = kvs[:, 1].reshape(TOKENS, HEAD_SIZE)
        grad = dctx[:, cols].astype(BF16)
        p = probs[head]
        prob_grad = dot(grad, value, 1, 1)
        delta = jnp.sum(prob_grad * p, axis=1, keepdims=True)
        score_grad = (p * (prob_grad - delta)).astype(BF16)
        o_q[:, cols] = (dot(score_grad, key, 1, 0) * scale).astype(BF16)
        return dot(score_grad, q_ref[:, cols], 0, 0) * scale, dot(p.astype(BF16), grad, 0, 0)

    def kv_place(t):
        lanes = pl.ds(pl.multiple_of(lax.div(t, 4) * HEAD_SIZE, HEAD_SIZE), HEAD_SIZE)
        return o_kv.at[lax.rem(t, 4), :, :, lanes]

    def kv_steps(*pairs):
        for s, j in pairs:
            gather_step(kv_place, kvsem, s, j)

    pl.semaphore_wait(barrier, len(partners))

    for k in (1, -1):
        send(c_own, c_place(ti), bsem.at[ti], on_y[k])
    send(c_own, c_place(ti), bsem.at[ti], on_zl[1])
    for k in (1, 2):
        send(w_own, w_place(dpi), asem.at[dpi], on_zh[k])
    for k in (1, -1):
        send(w_own, w_place(dpi), asem.at[dpi], on_x[k])
    send(w_own, w_place(dpi), asem.at[dpi], other)
    for j in (2, 3):
        send(c_own, c_place(ti), bsem.at[ti], on_zl[j])

    load.wait()
    mask()
    attend(0)
    c_steps(1)
    attend(1)
    c_steps(2)
    w_x_all(zh)
    c_steps(3, 4)
    for k in (1, 2):
        d = (x * 3 + zhk[k]) * 2 + core
        arrive(w_place(d), asem.at[d])
        for m in (1, -1):
            send(w_place(d), w_place(d), asem.at[d], on_x[m])
        send(w_place(d), w_place(d), asem.at[d], other)
    c_steps(5, 6)
    w_x_all(zhk[1])
    c_steps(7, 8)
    w_x_all(zhk[2])
    for xd in range(4):
        for zd in range(3):
            d = (xd * 3 + zd) * 2 + 1 - core
            arrive(w_place(d), asem.at[d])

    lax.fori_loop(0, BLOCKS // 8, project, 0)
    ring_first()
    c_steps(9, 10)

    for xd in (x_at(2), x_at(way), x_at(-way), x):
        grad_share(xd)
    dctx[...] = jnp.zeros_like(dctx)
    lax.fori_loop(0, BLOCKS // 16, back, 0)
    ring_step(1)
    key_a, value_a = attend_back(0)
    key_b, value_b = attend_back(1)
    d_own[:, 0] = (key_a + key_b).astype(BF16).reshape(4, 64, HEAD_SIZE)
    d_own[:, 1] = (value_a + value_b).astype(BF16).reshape(4, 64, HEAD_SIZE)
    for j in (1, 2, 3):
        send(d_own.at[zlj[j]], dz.at[j], dzsem.at[j], on_zl[j])

    grad_sum(x_at(2))
    for zd in range(3):
        send(es.at[x_at(2) * 3 + zd], ex0.at[zd], exsem.at[zd], on_x[1])
    grad_sum(x_at(-way))
    for zd in range(3):
        send(es.at[x_at(-way) * 3 + zd], ex2.at[zd], exsem.at[6 + zd], on_x[-1])
    ring_step(2)

    total = d_own[zl].astype(F32)
    for j in (1, 2, 3):
        arrive(dz.at[j], dzsem.at[j])
        total = total + dz[j].astype(F32)
    d_sum = total.astype(BF16)
    dz[0] = d_sum
    o_kv[zl, :, :, pl.ds(pl.multiple_of(y * HEAD_SIZE, HEAD_SIZE), HEAD_SIZE)] = d_sum
    for k in (1, -1):
        send(dz.at[0], kv_place(ti), kvsem.at[ti], on_y[k])
    for j in (1, 2, 3):
        send(dz.at[0], kv_place(ti), kvsem.at[ti], on_zl[j])

    grad_sum(x_at(way))
    for zd in range(3):
        c12 = x_at(way) * 3 + zd
        arrive(ex0.at[zd], exsem.at[zd])
        ex0[zd] = (ex0[zd].astype(F32) + es[c12].astype(F32)).astype(BF16)
        send(ex0.at[zd], ex1.at[zd], exsem.at[3 + zd], on_x[1])
    grad_sum(x)
    ring_step(3)

    kv_steps((0, 1), (0, 2), (0, 3), (1, 0))

    for zd in range(3):
        arrive(ex1.at[zd], exsem.at[3 + zd])
        arrive(ex2.at[zd], exsem.at[6 + zd])

    def arrived(zd):
        return es[x * 3 + zd].astype(F32) + ex1[zd].astype(F32) + ex2[zd].astype(F32)

    for k in (1, 2):
        fe[k] = arrived(zhk[k]).astype(BF16)
        send(fe.at[k], ez.at[k], ezsem.at[k], on_zh[k])

    for j in (1, 2, 3):
        fz[j] = ring_last(j).astype(BF16)
        send(fz.at[j], cz.at[j], czsem.at[j], on_zl[j])

    kv_steps((1, 1), (2, 0), (1, 2), (2, 1), (1, 3), (3, 0))
    acc = ring_last(0)
    w_sum = arrived(zh)
    kv_steps((2, 2), (3, 1), (2, 3), (3, 2), (3, 3))

    for j in (1, 2, 3):
        arrive(cz.at[j], czsem.at[j])
        acc = acc + cz[j].astype(F32)
    acc = acc.reshape(C_BLOCKS * ROWS, TOKENS)
    left = acc
    out = res_ref[...].astype(F32)
    turned = None
    for _ in range(3):
        part = left.astype(BF16)
        left = left - part.astype(F32)
        piece = dot(part, c_hot, 0, 0)
        turned = piece if turned is None else turned + piece
    o_res[...] = (out + turned).astype(BF16)

    for k in (1, 2):
        arrive(ez.at[k], ezsem.at[k])
        w_sum = w_sum + ez[k].astype(F32)
    for block in range(W_BLOCKS):
        o_w[pl.ds(block * REAL, REAL), :] = w_sum[block, :REAL]

    kv_steps((4, 0), (4, 1), (4, 2), (4, 3))

    for copy in sends:
        copy.wait_send()


def exchange(cot, w, q, kv, seg, res, live, counts):
    c_shape = (C_BLOCKS, ROWS, TOKENS)
    w_shape = (W_BLOCKS, ROWS, TOKENS)
    d_shape = (4, 2, 64, HEAD_SIZE)
    vmem = pl.BlockSpec(memory_space=pltpu.VMEM)
    smem = pl.BlockSpec(memory_space=pltpu.SMEM)
    dma = pltpu.SemaphoreType.DMA
    return pl.pallas_call(
        kernel,
        out_shape=(
            jax.ShapeDtypeStruct(res.shape, BF16),
            jax.ShapeDtypeStruct(q.shape, BF16),
            jax.ShapeDtypeStruct(kv.shape, BF16),
            jax.ShapeDtypeStruct(w.shape, F32),
        ),
        in_specs=[vmem, vmem, vmem, pl.BlockSpec(memory_space=pl.ANY), vmem, vmem, smem, smem],
        out_specs=(vmem, vmem, vmem, vmem),
        scratch_shapes=[
            pltpu.VMEM(c_shape, BF16),
            pltpu.VMEM(w_shape, BF16),
            pltpu.VMEM((BLOCKS, ROWS, TOKENS), BF16),
            pltpu.VMEM((BLOCKS, ROWS, TOKENS), BF16),
            pltpu.VMEM((BLOCKS, ROWS, TOKENS), BF16),
            pltpu.VMEM((16, *c_shape), BF16),
            pltpu.VMEM((16, *c_shape), BF16),
            pltpu.VMEM((4, *c_shape), BF16),
            pltpu.VMEM((4, *c_shape), BF16),
            pltpu.VMEM((12, *w_shape), BF16),
            pltpu.VMEM((12, *w_shape), BF16),
            pltpu.VMEM((12, *w_shape), BF16),
            pltpu.VMEM((3, *w_shape), BF16),
            pltpu.VMEM((3, *w_shape), BF16),
            pltpu.VMEM((3, *w_shape), BF16),
            pltpu.VMEM((3, *w_shape), BF16),
            pltpu.VMEM((3, *w_shape), BF16),
            pltpu.VMEM(d_shape, BF16),
            pltpu.VMEM(d_shape, BF16),
            pltpu.VMEM(d_shape, BF16),
            pltpu.VMEM((TOKENS, TOKENS), BF16),
            pltpu.VMEM((TOKENS, TOKENS), F32),
            pltpu.VMEM((2, TOKENS, TOKENS), F32),
            pltpu.VMEM((TOKENS, TOKENS), F32),
            dma((N_SEND,)),
            dma((32,)),
            dma((24,)),
            dma((16,)),
            dma((16,)),
            dma((4,)),
            dma((12,)),
            dma((9,)),
            dma((3,)),
            dma((4,)),
            dma((32,)),
            dma(()),
        ],
        compiler_params=pltpu.CompilerParams(
            collective_id=0, has_side_effects=True, vmem_limit_bytes=48 * 1024 * 1024
        ),
    )(cot, w, q, kv, seg, res, live, counts)


def per_device(
    queries, slot_keys_values, segment_ids, residual_in, cotangent, out_weight, live_mask, micro_counts
):
    res, q_grad, kv_grad, w_grad = exchange(
        cotangent.reshape(TOKENS, -1), out_weight.T, queries.reshape(TOKENS, TOKENS),
        slot_keys_values[0], segment_ids[0], residual_in.reshape(TOKENS, -1), live_mask, micro_counts,
    )
    return (
        res.reshape(residual_in.shape), q_grad.reshape(queries.shape), kv_grad[None], w_grad.T
    )


def solution(mesh):
    placed = (
        P("dp", None, None, "tensor"),
        P("dp", None, None, None, None),
        P("dp", None, None),
        P("dp", None, None, "tensor"),
        P("dp", None, None, "tensor"),
        P("tensor", "dp"),
        P(),
        P(),
    )
    return jax.shard_map(
        per_device,
        mesh=mesh,
        in_specs=placed,
        out_specs=(
            P("dp", None, None, "tensor"),
            P("dp", None, None, "tensor"),
            P("dp", None, None, None, None),
            P("tensor", "dp"),
        ),
        check_vma=False,
    )
```

```python
import math

import jax
import jax.numpy as jnp
from jax import lax
from jax.experimental import pallas as pl
from jax.experimental.pallas import tpu as pltpu
from jax.sharding import PartitionSpec as P

HEAD_SIZE = 128
MESH = pl.DeviceIdType.MESH
F32 = jnp.float32
BF16 = jnp.bfloat16

BLOCKS = 96
REAL = 44
ROWS = 48
C_BLOCKS = 3
W_BLOCKS = 4
TOKENS = 256
N_SEND = 176


def dot(a, b, ca, cb):
    return lax.dot_general(a, b, (((ca,), (cb,)), ((), ())), preferred_element_type=F32)


def one_hot(rows, cols):
    row = lax.broadcasted_iota(jnp.int32, (rows, cols), 0)
    col = lax.broadcasted_iota(jnp.int32, (rows, cols), 1)
    offset = lax.rem(row, ROWS)
    return jnp.where((col == lax.div(row, ROWS) * REAL + offset) & (offset < REAL), 1.0, 0.0).astype(BF16)


def kernel(
    cot_hbm, w_hbm, q_hbm, kv_hbm, seg_hbm, res_hbm, live_ref, count_ref,
    o_res, o_q, o_kv, o_w,
    cot_ref, w_ref, q_ref, seg_ref, res_ref, c_own, w_own, cg, wg, po, rp, rm, fz, cz, e_send, e_core, es, ex0, ex1, ex2, fe, ez,
    d_own, dz, kvs, ctx, bias, probs, dctx,
    ssem, bsem, asem, rpsem, rmsem, czsem, ecsem, exsem, ezsem, dzsem, kvsem, ldsem,
):
    dpi = lax.axis_index("dp")
    ti = lax.axis_index("tensor")
    core = lax.rem(dpi, 2)
    zh = lax.rem(lax.div(dpi, 2), 3)
    x = lax.div(dpi, 6)
    zl = lax.rem(ti, 4)
    y = lax.div(ti, 4)
    way = 1 - 2 * core

    def y_at(k):
        return lax.rem(y + (k + 8), 8)

    def x_at(k):
        return lax.rem(x + k + 4, 4)

    zlj = [zl, zl + 1 - 2 * lax.rem(zl, 2), lax.rem(zl + 2, 4), 3 - zl]
    zhk = [zh, lax.rem(zh + 1, 3), lax.rem(zh + 2, 3)]
    on_y = {k: (dpi, y_at(k) * 4 + zl) for k in (1, -1)}
    on_zl = [None] + [(dpi, y * 4 + zlj[j]) for j in (1, 2, 3)]
    on_zh = [None] + [((x * 3 + zhk[k]) * 2 + core, ti) for k in (1, 2)]
    on_x = {k: ((x_at(k * way) * 3 + zh) * 2 + core, ti) for k in (1, -1)}
    other = (dpi + way, ti)

    sends = []

    def send(src, dst, sem, device):
        copy = pltpu.make_async_remote_copy(
            src_ref=src, dst_ref=dst, send_sem=ssem.at[len(sends)], recv_sem=sem,
            device_id=device, device_id_type=MESH,
        )
        copy.start()
        sends.append(copy)

    def arrive(dst, sem):
        pltpu.make_async_remote_copy(
            src_ref=dst, dst_ref=dst, send_sem=ssem.at[0], recv_sem=sem,
            device_id=other, device_id_type=MESH,
        ).wait_recv()

    keys_values = kv_hbm.at[:, :, :, pl.ds(pl.multiple_of(y * HEAD_SIZE, HEAD_SIZE), HEAD_SIZE)]
    loads = [
        pltpu.make_async_copy(src, dst, ldsem.at[i])
        for i, (src, dst) in enumerate((
            (cot_hbm, cot_ref), (w_hbm, w_ref), (keys_values, kvs),
            (q_hbm, q_ref), (seg_hbm, seg_ref), (res_hbm, res_ref),
        ))
    ]
    for load in loads:
        load.start()

    partners = [on_y[1], on_y[-1], *on_zl[1:], *on_zh[1:], on_x[1], on_x[-1], other]
    barrier = pltpu.get_barrier_semaphore()
    for partner in partners:
        pl.semaphore_signal(barrier, inc=1, device_id=partner, device_id_type=MESH)

    units = 0
    for r in range(live_ref.shape[0]):
        units = units + live_ref[r] * count_ref[r]
    slot = lax.div(lax.broadcasted_iota(jnp.int32, (TOKENS, 1), 0), 64)
    counted = jnp.where(slot < count_ref[dpi], 1, 0) * jnp.where(live_ref[dpi] > 0, 1, 0)
    weight = counted.astype(F32) / jnp.full((TOKENS, 1), jnp.maximum(units, 1), jnp.int32).astype(F32)
    loads[0].wait()
    scaled = (cot_ref[...].astype(F32) * weight).astype(BF16)
    c_hot = one_hot(C_BLOCKS * ROWS, cot_ref.shape[1])
    c_block = dot(c_hot, scaled, 1, 1).astype(BF16).reshape(C_BLOCKS, ROWS, TOKENS)
    c_own[...] = c_block
    cg[pl.ds(ti * C_BLOCKS, C_BLOCKS)] = c_block
    loads[1].wait()
    w_block = dot(one_hot(W_BLOCKS * ROWS, w_ref.shape[0]), w_ref[...], 1, 0)
    w_block = w_block.astype(BF16).reshape(W_BLOCKS, ROWS, TOKENS)
    w_own[...] = w_block
    wg[pl.ds(dpi * W_BLOCKS, W_BLOCKS)] = w_block

    def c_place(t):
        return cg.at[pl.ds(t * C_BLOCKS, C_BLOCKS)]

    def w_half(d, h):
        return wg.at[pl.ds(d * W_BLOCKS + 2 * h, 2)], asem.at[2 * d + h]

    scale = 1.0 / math.sqrt(HEAD_SIZE)

    def mask():
        row = lax.broadcasted_iota(jnp.int32, (TOKENS, TOKENS), 0)
        col = lax.broadcasted_iota(jnp.int32, (TOKENS, TOKENS), 1)
        at = lax.broadcasted_iota(jnp.int32, (64, TOKENS), 0)
        token = lax.broadcasted_iota(jnp.int32, (64, TOKENS), 1)
        tile = jnp.where(lax.rem(token, 64) == at, 1.0, 0.0).astype(BF16)
        seg = seg_ref[...].astype(F32).astype(BF16)
        across = dot(seg, tile, 1, 0)
        down = dot(tile, seg, 0, 1)
        keep = lax.div(lax.broadcasted_iota(jnp.int32, (4, TOKENS), 1), 64)
        keep = keep == lax.broadcasted_iota(jnp.int32, (4, TOKENS), 0)
        seg_row = jnp.sum(jnp.where(keep, across, 0.0), axis=0, keepdims=True)
        keep = lax.div(lax.broadcasted_iota(jnp.int32, (TOKENS, 4), 0), 64)
        keep = keep == lax.broadcasted_iota(jnp.int32, (TOKENS, 4), 1)
        seg_col = jnp.sum(jnp.where(keep, down, 0.0), axis=1, keepdims=True)
        allowed = (col <= row) & (lax.div(col, 64) == lax.div(row, 64)) & (seg_col == seg_row)
        bias[...] = jnp.where(allowed, 0.0, -1e30)

    def attend(head):
        cols = slice(head * HEAD_SIZE, (head + 1) * HEAD_SIZE)
        key = kvs[:, 0].reshape(TOKENS, HEAD_SIZE)
        value = kvs[:, 1].reshape(TOKENS, HEAD_SIZE)
        scores = dot(q_ref[:, cols], key, 1, 1) * scale + bias[...]
        top = jnp.max(scores, axis=1, keepdims=True)
        expo = jnp.exp(scores - top)
        p = expo / jnp.sum(expo, axis=1, keepdims=True)
        probs[head] = p
        ctx[:, cols] = dot(p.astype(BF16), value, 1, 0).astype(BF16)

    def gather_step(place, sem, s, j):
        if s == 0:
            t = y * 4 + zlj[j]
            arrive(place(t), sem.at[t])
            for k in (1, -1):
                send(place(t), place(t), sem.at[t], on_y[k])
            return
        for k, mine in ((1, j < 2), (-1, j >= 2)):
            if s == 4 and not mine:
                continue
            t = y_at(-k * s) * 4 + zlj[j]
            arrive(place(t), sem.at[t])
            if s < 3 or (s == 3 and mine):
                send(place(t), place(t), sem.at[t], on_y[k])

    steps = {n: [] for n in range(1, 12)}
    for s in (4, 3, 2, 1, 0):
        for j in range(4):
            if s + j > 0:
                steps[2 * s + j].append((s, j))

    def c_steps(*ns):
        for n in ns:
            for s, j in steps[n]:
                gather_step(c_place, bsem, s, j)

    def w_pass(d, h, *devices):
        block, sem = w_half(d, h)
        arrive(block, sem)
        for device in devices:
            send(block, block, sem, device)

    def w_from(d_x, zhx):
        return (d_x * 3 + zhx) * 2 + core

    def w_near(zhx, h):
        w_pass(w_from(x_at(-way), zhx), h, on_x[1], other)
        w_pass(w_from(x_at(way), zhx), h, other)

    def w_far(zhx, h):
        w_pass(w_from(x_at(2), zhx), h, other)

    def w_z(h):
        for k in (1, 2):
            w_pass(w_from(x, zhk[k]), h, on_x[1], on_x[-1], other)

    def project(i, carry):
        n = 8
        out = dot(wg[pl.ds(i * n, n)].reshape(n * ROWS, TOKENS), ctx[...], 1, 1)
        po[pl.ds(i * n, n)] = out.astype(BF16).reshape(n, ROWS, TOKENS)
        return carry

    recv_buf = {1: (rp, rpsem), -1: (rm, rmsem)}

    def p_at(k, j):
        return po.at[pl.ds((y_at(k) * 4 + zlj[j]) * C_BLOCKS, C_BLOCKS)]

    def ring_slot(k, r, j):
        buf, sem = recv_buf[k]
        i = (r - 1) * 4 + j
        return buf.at[i], sem.at[i]

    def starts(k, j):
        return (j < 2) if k == 1 else (j >= 2)

    def ring_first():
        for j in range(4):
            for k in (1, -1):
                if starts(k, j):
                    send(p_at(4, j), *ring_slot(k, 1, j), on_y[k])
        for j in range(4):
            for k in (1, -1):
                if not starts(k, j):
                    send(p_at(3 * k, j), *ring_slot(k, 2, j), on_y[k])

    def ring_step(r):
        for j in range(4):
            for k in (1, -1):
                if r == 1 and not starts(k, j):
                    continue
                buf, _ = recv_buf[k]
                i = (r - 1) * 4 + j
                arrive(*ring_slot(k, r, j))
                own = po[pl.ds((y_at(k * (4 - r)) * 4 + zlj[j]) * C_BLOCKS, C_BLOCKS)]
                buf[i] = (buf[i].astype(F32) + own.astype(F32)).astype(BF16)
                send(ring_slot(k, r, j)[0], *ring_slot(k, r + 1, j), on_y[k])

    def ring_last(j):
        acc = po[pl.ds((y * 4 + zlj[j]) * C_BLOCKS, C_BLOCKS)].astype(F32)
        for k in (1, -1):
            arrive(*ring_slot(k, 4, j))
            acc = acc + recv_buf[k][0][12 + j].astype(F32)
        return acc

    def grad_chunk(d):
        return dot(cg[pl.ds(d * W_BLOCKS, W_BLOCKS)].reshape(W_BLOCKS * ROWS, TOKENS), ctx[...], 1, 0)

    def grad_share(xd):
        for zd in range(3):
            c12 = xd * 3 + zd
            part = grad_chunk(c12 * 2 + 1 - core).astype(BF16)
            e_send[c12] = part.reshape(W_BLOCKS, ROWS, TOKENS)
            send(e_send.at[c12], e_core.at[c12], ecsem.at[c12], other)

    def grad_sum(xd):
        for zd in range(3):
            c12 = xd * 3 + zd
            part = grad_chunk(c12 * 2 + core)
            arrive(e_core.at[c12], ecsem.at[c12])
            part = part.reshape(W_BLOCKS, ROWS, TOKENS) + e_core[c12].astype(F32)
            es[c12] = part.astype(BF16)

    def back(i, carry):
        n = 16
        dctx[...] += dot(
            cg[pl.ds(i * n, n)].reshape(n * ROWS, TOKENS),
            wg[pl.ds(i * n, n)].reshape(n * ROWS, TOKENS), 0, 0,
        )
        return carry

    def attend_back(head):
        cols = slice(head * HEAD_SIZE, (head + 1) * HEAD_SIZE)
        key = kvs[:, 0].reshape(TOKENS, HEAD_SIZE)
        value = kvs[:, 1].reshape(TOKENS, HEAD_SIZE)
        grad = dctx[:, cols].astype(BF16)
        p = probs[head]
        prob_grad = dot(grad, value, 1, 1)
        delta = jnp.sum(prob_grad * p, axis=1, keepdims=True)
        score_grad = (p * (prob_grad - delta)).astype(BF16)
        o_q[:, cols] = (dot(score_grad, key, 1, 0) * scale).astype(BF16)
        return dot(score_grad, q_ref[:, cols], 0, 0) * scale, dot(p.astype(BF16), grad, 0, 0)

    def kv_place(t):
        lanes = pl.ds(pl.multiple_of(lax.div(t, 4) * HEAD_SIZE, HEAD_SIZE), HEAD_SIZE)
        return o_kv.at[lax.rem(t, 4), :, :, lanes]

    def kv_steps(*pairs):
        for s, j in pairs:
            gather_step(kv_place, kvsem, s, j)

    pl.semaphore_wait(barrier, len(partners))

    for device in (on_y[1], on_y[-1], *on_zl[1:]):
        send(c_own, c_place(ti), bsem.at[ti], device)
    for h in (0, 1):
        for device in (on_x[1], on_x[-1], other):
            send(w_own.at[pl.ds(2 * h, 2)], *w_half(dpi, h), device)

    for load in loads[2:]:
        load.wait()
    mask()
    attend(0)
    c_steps(1)
    attend(1)
    c_steps(2)
    c_steps(3)
    for h in (0, 1):
        for device in on_zh[1:]:
            send(w_own.at[pl.ds(2 * h, 2)], *w_half(dpi, h), device)
    w_near(zh, 0)
    w_near(zh, 1)
    c_steps(4)
    w_far(zh, 0)
    w_far(zh, 1)
    c_steps(5)
    w_z(0)
    c_steps(6)
    for k in (1, 2):
        w_near(zhk[k], 0)
    c_steps(7)
    w_z(1)
    for k in (1, 2):
        w_far(zhk[k], 0)
    c_steps(8)
    for k in (1, 2):
        w_near(zhk[k], 1)
    c_steps(9)
    for k in (1, 2):
        w_far(zhk[k], 1)
    for xd in range(4):
        for zd in range(3):
            for h in (0, 1):
                arrive(*w_half((xd * 3 + zd) * 2 + 1 - core, h))

    lax.fori_loop(0, BLOCKS // 8, project, 0)
    ring_first()
    c_steps(10, 11)

    for xd in (x_at(2), x_at(way), x_at(-way), x):
        grad_share(xd)
    dctx[...] = jnp.zeros_like(dctx)
    lax.fori_loop(0, BLOCKS // 16, back, 0)
    ring_step(1)
    key_a, value_a = attend_back(0)
    key_b, value_b = attend_back(1)
    d_own[:, 0] = (key_a + key_b).astype(BF16).reshape(4, 64, HEAD_SIZE)
    d_own[:, 1] = (value_a + value_b).astype(BF16).reshape(4, 64, HEAD_SIZE)
    for j in (1, 2, 3):
        send(d_own.at[zlj[j]], dz.at[j], dzsem.at[j], on_zl[j])

    grad_sum(x_at(2))
    for zd in range(3):
        send(es.at[x_at(2) * 3 + zd], ex0.at[zd], exsem.at[zd], on_x[1])
    grad_sum(x_at(-way))
    for zd in range(3):
        send(es.at[x_at(-way) * 3 + zd], ex2.at[zd], exsem.at[6 + zd], on_x[-1])
    ring_step(2)

    total = d_own[zl].astype(F32)
    for j in (1, 2, 3):
        arrive(dz.at[j], dzsem.at[j])
        total = total + dz[j].astype(F32)
    d_sum = total.astype(BF16)
    dz[0] = d_sum
    o_kv[zl, :, :, pl.ds(pl.multiple_of(y * HEAD_SIZE, HEAD_SIZE), HEAD_SIZE)] = d_sum
    for k in (1, -1):
        send(dz.at[0], kv_place(ti), kvsem.at[ti], on_y[k])
    for j in (1, 2, 3):
        send(dz.at[0], kv_place(ti), kvsem.at[ti], on_zl[j])

    grad_sum(x_at(way))
    for zd in range(3):
        c12 = x_at(way) * 3 + zd
        arrive(ex0.at[zd], exsem.at[zd])
        ex0[zd] = (ex0[zd].astype(F32) + es[c12].astype(F32)).astype(BF16)
        send(ex0.at[zd], ex1.at[zd], exsem.at[3 + zd], on_x[1])
    grad_sum(x)
    ring_step(3)

    kv_steps((0, 1), (0, 2), (0, 3), (1, 0))

    for zd in range(3):
        arrive(ex1.at[zd], exsem.at[3 + zd])
        arrive(ex2.at[zd], exsem.at[6 + zd])

    def arrived(zd):
        return es[x * 3 + zd].astype(F32) + ex1[zd].astype(F32) + ex2[zd].astype(F32)

    for k in (1, 2):
        fe[k] = arrived(zhk[k]).astype(BF16)
        send(fe.at[k], ez.at[k], ezsem.at[k], on_zh[k])

    for j in (1, 2, 3):
        fz[j] = ring_last(j).astype(BF16)
        send(fz.at[j], cz.at[j], czsem.at[j], on_zl[j])

    kv_steps((1, 1), (2, 0), (1, 2), (2, 1), (1, 3), (3, 0))
    acc = ring_last(0)
    w_sum = arrived(zh)
    kv_steps((2, 2), (3, 1), (2, 3), (3, 2), (3, 3))

    for j in (1, 2, 3):
        arrive(cz.at[j], czsem.at[j])
        acc = acc + cz[j].astype(F32)
    acc = acc.reshape(C_BLOCKS * ROWS, TOKENS)
    left = acc
    out = res_ref[...].astype(F32)
    turned = None
    for _ in range(3):
        part = left.astype(BF16)
        left = left - part.astype(F32)
        piece = dot(part, c_hot, 0, 0)
        turned = piece if turned is None else turned + piece
    o_res[...] = (out + turned).astype(BF16)

    for k in (1, 2):
        arrive(ez.at[k], ezsem.at[k])
        w_sum = w_sum + ez[k].astype(F32)
    for block in range(W_BLOCKS):
        o_w[pl.ds(block * REAL, REAL), :] = w_sum[block, :REAL]

    kv_steps((4, 0), (4, 1), (4, 2), (4, 3))

    for copy in sends:
        copy.wait_send()


def exchange(cot, w, q, kv, seg, res, live, counts):
    c_shape = (C_BLOCKS, ROWS, TOKENS)
    w_shape = (W_BLOCKS, ROWS, TOKENS)
    d_shape = (4, 2, 64, HEAD_SIZE)
    vmem = pl.BlockSpec(memory_space=pltpu.VMEM)
    hbm = pl.BlockSpec(memory_space=pl.ANY)
    smem = pl.BlockSpec(memory_space=pltpu.SMEM)
    dma = pltpu.SemaphoreType.DMA
    return pl.pallas_call(
        kernel,
        out_shape=(
            jax.ShapeDtypeStruct(res.shape, BF16),
            jax.ShapeDtypeStruct(q.shape, BF16),
            jax.ShapeDtypeStruct(kv.shape, BF16),
            jax.ShapeDtypeStruct(w.shape, F32),
        ),
        in_specs=[hbm] * 6 + [smem] * 2,
        out_specs=(vmem, vmem, vmem, vmem),
        scratch_shapes=[
            pltpu.VMEM(cot.shape, BF16),
            pltpu.VMEM(w.shape, BF16),
            pltpu.VMEM(q.shape, BF16),
            pltpu.VMEM(seg.shape, jnp.int32),
            pltpu.VMEM(res.shape, BF16),
            pltpu.VMEM(c_shape, BF16),
            pltpu.VMEM(w_shape, BF16),
            pltpu.VMEM((BLOCKS, ROWS, TOKENS), BF16),
            pltpu.VMEM((BLOCKS, ROWS, TOKENS), BF16),
            pltpu.VMEM((BLOCKS, ROWS, TOKENS), BF16),
            pltpu.VMEM((16, *c_shape), BF16),
            pltpu.VMEM((16, *c_shape), BF16),
            pltpu.VMEM((4, *c_shape), BF16),
            pltpu.VMEM((4, *c_shape), BF16),
            pltpu.VMEM((12, *w_shape), BF16),
            pltpu.VMEM((12, *w_shape), BF16),
            pltpu.VMEM((12, *w_shape), BF16),
            pltpu.VMEM((3, *w_shape), BF16),
            pltpu.VMEM((3, *w_shape), BF16),
            pltpu.VMEM((3, *w_shape), BF16),
            pltpu.VMEM((3, *w_shape), BF16),
            pltpu.VMEM((3, *w_shape), BF16),
            pltpu.VMEM(d_shape, BF16),
            pltpu.VMEM(d_shape, BF16),
            pltpu.VMEM(d_shape, BF16),
            pltpu.VMEM((TOKENS, TOKENS), BF16),
            pltpu.VMEM((TOKENS, TOKENS), F32),
            pltpu.VMEM((2, TOKENS, TOKENS), F32),
            pltpu.VMEM((TOKENS, TOKENS), F32),
            dma((N_SEND,)),
            dma((32,)),
            dma((48,)),
            dma((16,)),
            dma((16,)),
            dma((4,)),
            dma((12,)),
            dma((9,)),
            dma((3,)),
            dma((4,)),
            dma((32,)),
            dma((6,)),
        ],
        compiler_params=pltpu.CompilerParams(
            collective_id=0, has_side_effects=True, vmem_limit_bytes=60 * 1024 * 1024
        ),
    )(cot, w, q, kv, seg, res, live, counts)


def per_device(
    queries, slot_keys_values, segment_ids, residual_in, cotangent, out_weight, live_mask, micro_counts
):
    res, q_grad, kv_grad, w_grad = exchange(
        cotangent.reshape(TOKENS, -1), out_weight.T, queries.reshape(TOKENS, TOKENS),
        slot_keys_values[0], segment_ids[0], residual_in.reshape(TOKENS, -1), live_mask, micro_counts,
    )
    return (
        res.reshape(residual_in.shape), q_grad.reshape(queries.shape), kv_grad[None], w_grad.T
    )


def solution(mesh):
    placed = (
        P("dp", None, None, "tensor"),
        P("dp", None, None, None, None),
        P("dp", None, None),
        P("dp", None, None, "tensor"),
        P("dp", None, None, "tensor"),
        P("tensor", "dp"),
        P(),
        P(),
    )
    return jax.shard_map(
        per_device,
        mesh=mesh,
        in_specs=placed,
        out_specs=(
            P("dp", None, None, "tensor"),
            P("dp", None, None, "tensor"),
            P("dp", None, None, None, None),
            P("tensor", "dp"),
        ),
        check_vma=False,
    )
```

```python
import math

import jax
import jax.numpy as jnp
from jax import lax
from jax.experimental import pallas as pl
from jax.experimental.pallas import tpu as pltpu
from jax.sharding import PartitionSpec as P

HEAD_SIZE = 128
MESH = pl.DeviceIdType.MESH
F32 = jnp.float32
BF16 = jnp.bfloat16

BLOCKS = 96
REAL = 44
ROWS = 48
C_BLOCKS = 3
W_BLOCKS = 4
TOKENS = 256
N_SEND = 176


def dot(a, b, ca, cb):
    return lax.dot_general(a, b, (((ca,), (cb,)), ((), ())), preferred_element_type=F32)


def one_hot(rows, cols):
    row = lax.broadcasted_iota(jnp.int32, (rows, cols), 0)
    col = lax.broadcasted_iota(jnp.int32, (rows, cols), 1)
    offset = lax.rem(row, ROWS)
    return jnp.where((col == lax.div(row, ROWS) * REAL + offset) & (offset < REAL), 1.0, 0.0).astype(BF16)


def kernel(
    cot_hbm, w_hbm, q_hbm, kv_hbm, seg_hbm, res_hbm, live_ref, count_ref,
    o_res, o_q, o_kv, o_w,
    cot_ref, w_ref, q_ref, seg_ref, res_ref, c_own, w_own, cg, wg, po, rp, rm, fz, cz, e_send, e_core, es, ex0, ex1, ex2, fe, ez,
    d_own, dz, kvs, ctx, bias, probs, dctx,
    ssem, bsem, asem, rpsem, rmsem, czsem, ecsem, exsem, ezsem, dzsem, kvsem, ldsem,
):
    dpi = lax.axis_index("dp")
    ti = lax.axis_index("tensor")
    core = lax.rem(dpi, 2)
    zh = lax.rem(lax.div(dpi, 2), 3)
    x = lax.div(dpi, 6)
    zl = lax.rem(ti, 4)
    y = lax.div(ti, 4)
    way = 1 - 2 * core

    def y_at(k):
        return lax.rem(y + (k + 8), 8)

    def x_at(k):
        return lax.rem(x + k + 4, 4)

    zlj = [zl, zl + 1 - 2 * lax.rem(zl, 2), lax.rem(zl + 2, 4), 3 - zl]
    zhk = [zh, lax.rem(zh + 1, 3), lax.rem(zh + 2, 3)]
    on_y = {k: (dpi, y_at(k) * 4 + zl) for k in (1, -1)}
    on_zl = [None] + [(dpi, y * 4 + zlj[j]) for j in (1, 2, 3)]
    on_zh = [None] + [((x * 3 + zhk[k]) * 2 + core, ti) for k in (1, 2)]
    on_x = {k: ((x_at(k * way) * 3 + zh) * 2 + core, ti) for k in (1, -1)}
    other = (dpi + way, ti)

    sends = []

    def send(src, dst, sem, device):
        copy = pltpu.make_async_remote_copy(
            src_ref=src, dst_ref=dst, send_sem=ssem.at[len(sends)], recv_sem=sem,
            device_id=device, device_id_type=MESH,
        )
        copy.start()
        sends.append(copy)

    def arrive(dst, sem):
        pltpu.make_async_remote_copy(
            src_ref=dst, dst_ref=dst, send_sem=ssem.at[0], recv_sem=sem,
            device_id=other, device_id_type=MESH,
        ).wait_recv()

    keys_values = kv_hbm.at[:, :, :, pl.ds(pl.multiple_of(y * HEAD_SIZE, HEAD_SIZE), HEAD_SIZE)]
    loads = [
        pltpu.make_async_copy(src, dst, ldsem.at[i])
        for i, (src, dst) in enumerate((
            (cot_hbm, cot_ref), (w_hbm, w_ref), (keys_values, kvs),
            (q_hbm, q_ref), (seg_hbm, seg_ref), (res_hbm, res_ref),
        ))
    ]
    for load in loads:
        load.start()

    partners = [on_y[1], on_y[-1], *on_zl[1:], *on_zh[1:], on_x[1], on_x[-1], other]
    barrier = pltpu.get_barrier_semaphore()
    for partner in partners:
        pl.semaphore_signal(barrier, inc=1, device_id=partner, device_id_type=MESH)

    units = 0
    for r in range(live_ref.shape[0]):
        units = units + live_ref[r] * count_ref[r]
    slot = lax.div(lax.broadcasted_iota(jnp.int32, (TOKENS, 1), 0), 64)
    counted = jnp.where(slot < count_ref[dpi], 1, 0) * jnp.where(live_ref[dpi] > 0, 1, 0)
    weight = counted.astype(F32) / jnp.full((TOKENS, 1), jnp.maximum(units, 1), jnp.int32).astype(F32)
    loads[0].wait()
    scaled = (cot_ref[...].astype(F32) * weight).astype(BF16)
    c_hot = one_hot(C_BLOCKS * ROWS, cot_ref.shape[1])
    c_block = dot(c_hot, scaled, 1, 1).astype(BF16).reshape(C_BLOCKS, ROWS, TOKENS)
    c_own[...] = c_block
    cg[pl.ds(ti * C_BLOCKS, C_BLOCKS)] = c_block
    loads[1].wait()
    w_block = dot(one_hot(W_BLOCKS * ROWS, w_ref.shape[0]), w_ref[...], 1, 0)
    w_block = w_block.astype(BF16).reshape(W_BLOCKS, ROWS, TOKENS)
    w_own[...] = w_block
    wg[pl.ds(dpi * W_BLOCKS, W_BLOCKS)] = w_block

    def c_place(t):
        return cg.at[pl.ds(t * C_BLOCKS, C_BLOCKS)]

    def w_half(d, h):
        return wg.at[pl.ds(d * W_BLOCKS + 2 * h, 2)], asem.at[2 * d + h]

    scale = 1.0 / math.sqrt(HEAD_SIZE)

    def mask():
        row = lax.broadcasted_iota(jnp.int32, (TOKENS, TOKENS), 0)
        col = lax.broadcasted_iota(jnp.int32, (TOKENS, TOKENS), 1)
        at = lax.broadcasted_iota(jnp.int32, (64, TOKENS), 0)
        token = lax.broadcasted_iota(jnp.int32, (64, TOKENS), 1)
        tile = jnp.where(lax.rem(token, 64) == at, 1.0, 0.0).astype(BF16)
        seg = seg_ref[...].astype(F32).astype(BF16)
        across = dot(seg, tile, 1, 0)
        down = dot(tile, seg, 0, 1)
        keep = lax.div(lax.broadcasted_iota(jnp.int32, (4, TOKENS), 1), 64)
        keep = keep == lax.broadcasted_iota(jnp.int32, (4, TOKENS), 0)
        seg_row = jnp.sum(jnp.where(keep, across, 0.0), axis=0, keepdims=True)
        keep = lax.div(lax.broadcasted_iota(jnp.int32, (TOKENS, 4), 0), 64)
        keep = keep == lax.broadcasted_iota(jnp.int32, (TOKENS, 4), 1)
        seg_col = jnp.sum(jnp.where(keep, down, 0.0), axis=1, keepdims=True)
        allowed = (col <= row) & (lax.div(col, 64) == lax.div(row, 64)) & (seg_col == seg_row)
        bias[...] = jnp.where(allowed, 0.0, -1e30)

    def attend(head):
        cols = slice(head * HEAD_SIZE, (head + 1) * HEAD_SIZE)
        key = kvs[:, 0].reshape(TOKENS, HEAD_SIZE)
        value = kvs[:, 1].reshape(TOKENS, HEAD_SIZE)
        scores = dot(q_ref[:, cols], key, 1, 1) * scale + bias[...]
        top = jnp.max(scores, axis=1, keepdims=True)
        expo = jnp.exp(scores - top)
        p = expo / jnp.sum(expo, axis=1, keepdims=True)
        probs[head] = p
        ctx[:, cols] = dot(p.astype(BF16), value, 1, 0).astype(BF16)

    def gather_step(place, sem, s, j):
        if s == 0:
            t = y * 4 + zlj[j]
            arrive(place(t), sem.at[t])
            for k in (1, -1):
                send(place(t), place(t), sem.at[t], on_y[k])
            return
        for k, mine in ((1, j < 2), (-1, j >= 2)):
            if s == 4 and not mine:
                continue
            t = y_at(-k * s) * 4 + zlj[j]
            arrive(place(t), sem.at[t])
            if s < 3 or (s == 3 and mine):
                send(place(t), place(t), sem.at[t], on_y[k])

    steps = {n: [] for n in range(1, 12)}
    for s in (4, 3, 2, 1, 0):
        for j in range(4):
            if s + j > 0:
                steps[2 * s + j].append((s, j))

    def c_steps(*ns):
        for n in ns:
            for s, j in steps[n]:
                gather_step(c_place, bsem, s, j)

    def w_pass(d, h, *devices):
        block, sem = w_half(d, h)
        arrive(block, sem)
        for device in devices:
            send(block, block, sem, device)

    def w_from(d_x, zhx):
        return (d_x * 3 + zhx) * 2 + core

    def w_near(zhx, h):
        w_pass(w_from(x_at(-way), zhx), h, on_x[1], other)
        w_pass(w_from(x_at(way), zhx), h, other)

    def w_far(zhx, h):
        w_pass(w_from(x_at(2), zhx), h, other)

    def w_z(h):
        for k in (1, 2):
            w_pass(w_from(x, zhk[k]), h, on_x[1], on_x[-1], other)

    def project(i, carry):
        n = 8
        out = dot(wg[pl.ds(i * n, n)].reshape(n * ROWS, TOKENS), ctx[...], 1, 1)
        po[pl.ds(i * n, n)] = out.astype(BF16).reshape(n, ROWS, TOKENS)
        return carry

    def w_project(zhx):
        for d_x in range(4):
            for h in (0, 1):
                arrive(*w_half((d_x * 3 + zhx) * 2 + 1 - core, h))
        lax.fori_loop(0, 4, lambda d_x, carry: project(d_x * 3 + zhx, carry), 0)

    recv_buf = {1: (rp, rpsem), -1: (rm, rmsem)}

    def p_at(k, j):
        return po.at[pl.ds((y_at(k) * 4 + zlj[j]) * C_BLOCKS, C_BLOCKS)]

    def ring_slot(k, r, j):
        buf, sem = recv_buf[k]
        i = (r - 1) * 4 + j
        return buf.at[i], sem.at[i]

    def starts(k, j):
        return (j < 2) if k == 1 else (j >= 2)

    def ring_first():
        for j in (3, 2, 1, 0):
            for k in (1, -1):
                if starts(k, j):
                    send(p_at(4, j), *ring_slot(k, 1, j), on_y[k])
        for j in (3, 2, 1, 0):
            for k in (1, -1):
                if not starts(k, j):
                    send(p_at(3 * k, j), *ring_slot(k, 2, j), on_y[k])

    def ring_step(r):
        for j in (3, 2, 1, 0):
            for k in (1, -1):
                if r == 1 and not starts(k, j):
                    continue
                buf, _ = recv_buf[k]
                i = (r - 1) * 4 + j
                arrive(*ring_slot(k, r, j))
                own = po[pl.ds((y_at(k * (4 - r)) * 4 + zlj[j]) * C_BLOCKS, C_BLOCKS)]
                buf[i] = (buf[i].astype(F32) + own.astype(F32)).astype(BF16)
                send(ring_slot(k, r, j)[0], *ring_slot(k, r + 1, j), on_y[k])

    def ring_last(j):
        acc = po[pl.ds((y * 4 + zlj[j]) * C_BLOCKS, C_BLOCKS)].astype(F32)
        for k in (1, -1):
            arrive(*ring_slot(k, 4, j))
            acc = acc + recv_buf[k][0][12 + j].astype(F32)
        return acc

    def grad_chunk(d):
        return dot(cg[pl.ds(d * W_BLOCKS, W_BLOCKS)].reshape(W_BLOCKS * ROWS, TOKENS), ctx[...], 1, 0)

    def grad_share(xd):
        for zd in range(3):
            c12 = xd * 3 + zd
            part = grad_chunk(c12 * 2 + 1 - core).astype(BF16)
            e_send[c12] = part.reshape(W_BLOCKS, ROWS, TOKENS)
            send(e_send.at[c12], e_core.at[c12], ecsem.at[c12], other)

    def grad_sum(xd):
        for zd in range(3):
            c12 = xd * 3 + zd
            part = grad_chunk(c12 * 2 + core)
            arrive(e_core.at[c12], ecsem.at[c12])
            part = part.reshape(W_BLOCKS, ROWS, TOKENS) + e_core[c12].astype(F32)
            es[c12] = part.astype(BF16)

    def back(i, carry):
        n = 16
        dctx[...] += dot(
            cg[pl.ds(i * n, n)].reshape(n * ROWS, TOKENS),
            wg[pl.ds(i * n, n)].reshape(n * ROWS, TOKENS), 0, 0,
        )
        return carry

    def attend_back(head):
        cols = slice(head * HEAD_SIZE, (head + 1) * HEAD_SIZE)
        key = kvs[:, 0].reshape(TOKENS, HEAD_SIZE)
        value = kvs[:, 1].reshape(TOKENS, HEAD_SIZE)
        grad = dctx[:, cols].astype(BF16)
        p = probs[head]
        prob_grad = dot(grad, value, 1, 1)
        delta = jnp.sum(prob_grad * p, axis=1, keepdims=True)
        score_grad = (p * (prob_grad - delta)).astype(BF16)
        o_q[:, cols] = (dot(score_grad, key, 1, 0) * scale).astype(BF16)
        return dot(score_grad, q_ref[:, cols], 0, 0) * scale, dot(p.astype(BF16), grad, 0, 0)

    def kv_place(t):
        lanes = pl.ds(pl.multiple_of(lax.div(t, 4) * HEAD_SIZE, HEAD_SIZE), HEAD_SIZE)
        return o_kv.at[lax.rem(t, 4), :, :, lanes]

    def kv_steps(*pairs):
        for s, j in pairs:
            gather_step(kv_place, kvsem, s, j)

    pl.semaphore_wait(barrier, len(partners))

    for device in (on_y[1], on_y[-1], *on_zl[1:]):
        send(c_own, c_place(ti), bsem.at[ti], device)
    for h in (0, 1):
        for device in (on_x[1], on_x[-1], other):
            send(w_own.at[pl.ds(2 * h, 2)], *w_half(dpi, h), device)

    c_steps(1)
    c_steps(2)
    c_steps(3)
    for h in (0, 1):
        for device in on_zh[1:]:
            send(w_own.at[pl.ds(2 * h, 2)], *w_half(dpi, h), device)
    for load in loads[2:]:
        load.wait()
    mask()
    attend(0)
    w_near(zh, 0)
    w_near(zh, 1)
    c_steps(4)
    attend(1)
    w_far(zh, 0)
    w_far(zh, 1)
    c_steps(5)
    w_z(0)
    c_steps(6)
    for k in (1, 2):
        w_near(zhk[k], 0)
    c_steps(7)
    w_z(1)
    for k in (1, 2):
        w_far(zhk[k], 0)
    c_steps(8)
    w_project(zh)
    for k in (1, 2):
        w_near(zhk[k], 1)
    c_steps(9)
    for k in (1, 2):
        w_far(zhk[k], 1)
    for k in (1, 2):
        w_project(zhk[k])
    ring_first()
    c_steps(10, 11)

    for xd in (x_at(2), x_at(way), x_at(-way), x):
        grad_share(xd)
    dctx[...] = jnp.zeros_like(dctx)
    lax.fori_loop(0, BLOCKS // 16, back, 0)
    ring_step(1)
    key_a, value_a = attend_back(0)
    key_b, value_b = attend_back(1)
    d_own[:, 0] = (key_a + key_b).astype(BF16).reshape(4, 64, HEAD_SIZE)
    d_own[:, 1] = (value_a + value_b).astype(BF16).reshape(4, 64, HEAD_SIZE)
    for j in (1, 2, 3):
        send(d_own.at[zlj[j]], dz.at[j], dzsem.at[j], on_zl[j])

    grad_sum(x_at(2))
    for zd in range(3):
        send(es.at[x_at(2) * 3 + zd], ex0.at[zd], exsem.at[zd], on_x[1])
    grad_sum(x_at(-way))
    for zd in range(3):
        send(es.at[x_at(-way) * 3 + zd], ex2.at[zd], exsem.at[6 + zd], on_x[-1])
    ring_step(2)

    total = d_own[zl].astype(F32)
    for j in (1, 2, 3):
        arrive(dz.at[j], dzsem.at[j])
        total = total + dz[j].astype(F32)
    d_sum = total.astype(BF16)
    dz[0] = d_sum
    o_kv[zl, :, :, pl.ds(pl.multiple_of(y * HEAD_SIZE, HEAD_SIZE), HEAD_SIZE)] = d_sum
    for k in (1, -1):
        send(dz.at[0], kv_place(ti), kvsem.at[ti], on_y[k])
    for j in (1, 2, 3):
        send(dz.at[0], kv_place(ti), kvsem.at[ti], on_zl[j])

    grad_sum(x_at(way))
    for zd in range(3):
        c12 = x_at(way) * 3 + zd
        arrive(ex0.at[zd], exsem.at[zd])
        ex0[zd] = (ex0[zd].astype(F32) + es[c12].astype(F32)).astype(BF16)
        send(ex0.at[zd], ex1.at[zd], exsem.at[3 + zd], on_x[1])
    grad_sum(x)
    ring_step(3)

    kv_steps((0, 1), (0, 2), (0, 3), (1, 0))

    for zd in range(3):
        arrive(ex1.at[zd], exsem.at[3 + zd])
        arrive(ex2.at[zd], exsem.at[6 + zd])

    def arrived(zd):
        return es[x * 3 + zd].astype(F32) + ex1[zd].astype(F32) + ex2[zd].astype(F32)

    for k in (1, 2):
        fe[k] = arrived(zhk[k]).astype(BF16)
        send(fe.at[k], ez.at[k], ezsem.at[k], on_zh[k])

    for j in (3, 2, 1):
        fz[j] = ring_last(j).astype(BF16)
        send(fz.at[j], cz.at[j], czsem.at[j], on_zl[j])

    kv_steps((1, 1), (2, 0), (1, 2), (2, 1), (1, 3), (3, 0))
    acc = ring_last(0)
    w_sum = arrived(zh)
    kv_steps((2, 2), (3, 1), (2, 3), (3, 2), (3, 3))

    for j in (1, 2, 3):
        arrive(cz.at[j], czsem.at[j])
        acc = acc + cz[j].astype(F32)
    acc = acc.reshape(C_BLOCKS * ROWS, TOKENS)
    left = acc
    out = res_ref[...].astype(F32)
    turned = None
    for _ in range(3):
        part = left.astype(BF16)
        left = left - part.astype(F32)
        piece = dot(part, c_hot, 0, 0)
        turned = piece if turned is None else turned + piece
    o_res[...] = (out + turned).astype(BF16)

    for k in (1, 2):
        arrive(ez.at[k], ezsem.at[k])
        w_sum = w_sum + ez[k].astype(F32)
    for block in range(W_BLOCKS):
        o_w[pl.ds(block * REAL, REAL), :] = w_sum[block, :REAL]

    kv_steps((4, 0), (4, 1), (4, 2), (4, 3))

    for copy in sends:
        copy.wait_send()


def exchange(cot, w, q, kv, seg, res, live, counts):
    c_shape = (C_BLOCKS, ROWS, TOKENS)
    w_shape = (W_BLOCKS, ROWS, TOKENS)
    d_shape = (4, 2, 64, HEAD_SIZE)
    vmem = pl.BlockSpec(memory_space=pltpu.VMEM)
    hbm = pl.BlockSpec(memory_space=pl.ANY)
    smem = pl.BlockSpec(memory_space=pltpu.SMEM)
    dma = pltpu.SemaphoreType.DMA
    return pl.pallas_call(
        kernel,
        out_shape=(
            jax.ShapeDtypeStruct(res.shape, BF16),
            jax.ShapeDtypeStruct(q.shape, BF16),
            jax.ShapeDtypeStruct(kv.shape, BF16),
            jax.ShapeDtypeStruct(w.shape, F32),
        ),
        in_specs=[hbm] * 6 + [smem] * 2,
        out_specs=(vmem, vmem, vmem, vmem),
        scratch_shapes=[
            pltpu.VMEM(cot.shape, BF16),
            pltpu.VMEM(w.shape, BF16),
            pltpu.VMEM(q.shape, BF16),
            pltpu.VMEM(seg.shape, jnp.int32),
            pltpu.VMEM(res.shape, BF16),
            pltpu.VMEM(c_shape, BF16),
            pltpu.VMEM(w_shape, BF16),
            pltpu.VMEM((BLOCKS, ROWS, TOKENS), BF16),
            pltpu.VMEM((BLOCKS, ROWS, TOKENS), BF16),
            pltpu.VMEM((BLOCKS, ROWS, TOKENS), BF16),
            pltpu.VMEM((16, *c_shape), BF16),
            pltpu.VMEM((16, *c_shape), BF16),
            pltpu.VMEM((4, *c_shape), BF16),
            pltpu.VMEM((4, *c_shape), BF16),
            pltpu.VMEM((12, *w_shape), BF16),
            pltpu.VMEM((12, *w_shape), BF16),
            pltpu.VMEM((12, *w_shape), BF16),
            pltpu.VMEM((3, *w_shape), BF16),
            pltpu.VMEM((3, *w_shape), BF16),
            pltpu.VMEM((3, *w_shape), BF16),
            pltpu.VMEM((3, *w_shape), BF16),
            pltpu.VMEM((3, *w_shape), BF16),
            pltpu.VMEM(d_shape, BF16),
            pltpu.VMEM(d_shape, BF16),
            pltpu.VMEM(d_shape, BF16),
            pltpu.VMEM((TOKENS, TOKENS), BF16),
            pltpu.VMEM((TOKENS, TOKENS), F32),
            pltpu.VMEM((2, TOKENS, TOKENS), F32),
            pltpu.VMEM((TOKENS, TOKENS), F32),
            dma((N_SEND,)),
            dma((32,)),
            dma((48,)),
            dma((16,)),
            dma((16,)),
            dma((4,)),
            dma((12,)),
            dma((9,)),
            dma((3,)),
            dma((4,)),
            dma((32,)),
            dma((6,)),
        ],
        compiler_params=pltpu.CompilerParams(
            collective_id=0, has_side_effects=True, vmem_limit_bytes=60 * 1024 * 1024
        ),
    )(cot, w, q, kv, seg, res, live, counts)


def per_device(
    queries, slot_keys_values, segment_ids, residual_in, cotangent, out_weight, live_mask, micro_counts
):
    res, q_grad, kv_grad, w_grad = exchange(
        cotangent.reshape(TOKENS, -1), out_weight.T, queries.reshape(TOKENS, TOKENS),
        slot_keys_values[0], segment_ids[0], residual_in.reshape(TOKENS, -1), live_mask, micro_counts,
    )
    return (
        res.reshape(residual_in.shape), q_grad.reshape(queries.shape), kv_grad[None], w_grad.T
    )


def solution(mesh):
    placed = (
        P("dp", None, None, "tensor"),
        P("dp", None, None, None, None),
        P("dp", None, None),
        P("dp", None, None, "tensor"),
        P("dp", None, None, "tensor"),
        P("tensor", "dp"),
        P(),
        P(),
    )
    return jax.shard_map(
        per_device,
        mesh=mesh,
        in_specs=placed,
        out_specs=(
            P("dp", None, None, "tensor"),
            P("dp", None, None, "tensor"),
            P("dp", None, None, None, None),
            P("tensor", "dp"),
        ),
        check_vma=False,
    )
```
